128 devices in a mesh: rows: 32 (over z, y_lo, x), cols: 4 (over y_hi, core).
Axes of the slice: x: 4, y: 4 (y_hi: 2, y_lo: 2; y = y_hi * 2 + y_lo), z: 4, core: 2. Of those that a mesh axis runs over, the one named last changes fastest.
Arguments:
- field: bfloat16 [1, 18432, 18432], P(None, 'rows', 'cols'), may hold values from -48 to 48
Outputs:
- spectra: float32 [1, 1152, 2304], P(None, ('rows', 'cols'))
The draws below stay inside these ranges and needn't reach their ends.
All inputs are finite; a program needn't handle non-finite values.
Results may differ from the reference program's by a relative error of at most 0.0003.
The reference program's roundings to bfloat16 on the way (of `taps`) count: a program that leaves them out, or rounds other values in their place, can miss the bound.
Values may be sent and summed in bfloat16 or wider, within the bound.
A program may use at most 64 MiB of HBM per device.

```python
import jax
import jax.numpy as jnp
from jax import lax

FIELDS = 1
NK = 2304
TAPS = 33
STRIDE = 8
NY = 18432
KH = 1152


def steps_of(stream_key, shape, shards, smallest, high):
    def one(dim, shards_of):
        draws = jax.random.uniform(jax.random.fold_in(jax.random.fold_in(stream_key, 6), dim), (shards_of,), jnp.float32, smallest / len(shards), high / len(shards))
        return jnp.repeat(jnp.exp(draws), shape[dim] // shards_of).reshape((-1,) + (1,) * (len(shape) - dim - 1))

    gain = one(*shards[0])
    for cut in shards[1:]:
        gain = gain * one(*cut)
    return gain


def normal_values(own_key, dims, width, limit, shards=(), kind=jnp.bfloat16):
    array = jax.random.normal(own_key, dims, jnp.float32) * width
    if len(shards) > 0:
        array = steps_of(own_key, dims, shards, -0.22, 0.18) * array
    return jnp.clip(array, min=-limit, max=limit).astype(kind)


def setup_inputs(seed: int = 0) -> dict:
    key_list = jax.random.split(jax.random.key(seed), 2)
    return {
        "field": normal_values(key_list[0], (FIELDS, NY, NY), 8.0, 48.0, ((1, 32), (2, 4))),
    }


def taps_table():
    tap_ids = jnp.arange(TAPS, dtype=jnp.float32)
    centre = TAPS // 2
    shaped = jnp.sinc((tap_ids - centre) / STRIDE) * (0.54 - 0.46 * jnp.cos(2 * jnp.pi * tap_ids / (TAPS - 1)))
    shaped = shaped / jnp.sum(shaped)
    rounded = lax.optimization_barrier(shaped.astype(jnp.bfloat16))
    return rounded.astype(jnp.float32)


def one_field(plane):
    taps = taps_table()
    tap_reach = TAPS // 2
    padded = jnp.pad(plane, ((tap_reach, tap_reach), (0, 0)))
    rowcut = jnp.zeros((NK, NY), jnp.float32)
    for tap_id in range(TAPS):
        rowcut = rowcut + taps[tap_id] * padded[tap_id:tap_id + STRIDE * NK:STRIDE, :].astype(jnp.float32)
    padded_cut = jnp.pad(rowcut, ((0, 0), (tap_reach, tap_reach)))
    cut = jnp.zeros((NK, NK), jnp.float32)
    for tap_id in range(TAPS):
        cut = cut + taps[tap_id] * padded_cut[:, tap_id:tap_id + STRIDE * NK:STRIDE]
    points = jnp.arange(NK, dtype=jnp.float32)
    window = 0.5 - 0.5 * jnp.cos(2 * jnp.pi * points / NK)
    tapered = cut * window[:, None] * window[None, :]
    transform = jnp.fft.rfft2(tapered)[:, :KH]
    power = (jnp.real(transform) * jnp.real(transform) + jnp.imag(transform) * jnp.imag(transform)) * (8.0 / (NK * NK))
    return power.T


def reference(field):
    return lax.map(one_field, field)
```

```python
import math

import jax
import jax.numpy as jnp
from jax import lax
from jax.experimental import pallas as pl
from jax.experimental.pallas import tpu as pltpu
from jax.sharding import PartitionSpec as P

TAPS = 33
STRIDE = 8


def extended_2(shard, sides, width):
    for axis, dim in sides:
        count, length = (lax.axis_size(axis), shard.shape[dim])
        up = [(i, (i + 1) % count) for i in range(count - 1)]
        down = [(j, i) for i, j in up]
        last = lax.slice_in_dim(shard, length - width, length, axis=dim)
        initial = lax.slice_in_dim(shard, 0, width, axis=dim)
        before = lax.ppermute(last, axis, up)
        after = lax.ppermute(initial, axis, down)
        shard = jnp.concatenate([before, shard, after], axis=dim)
    return shard


def taps_table():
    tap_ids = jnp.arange(TAPS, dtype=jnp.float32)
    centre = TAPS // 2
    shaped = jnp.sinc((tap_ids - centre) / STRIDE) * (
        0.54 - 0.46 * jnp.cos(2 * jnp.pi * tap_ids / (TAPS - 1))
    )
    shaped = shaped / jnp.sum(shaped)
    rounded = lax.optimization_barrier(shaped.astype(jnp.bfloat16))
    return rounded.astype(jnp.float32)


def band_matrix(span_in, span_out, out_type):
    taps = taps_table()
    row_ids = lax.broadcasted_iota(jnp.int32, (span_in, span_out), 0)
    col_ids = lax.broadcasted_iota(jnp.int32, (span_in, span_out), 1)
    offset = row_ids - STRIDE * col_ids
    matrix = jnp.zeros((span_in, span_out), jnp.float32)
    for tap_id in range(TAPS):
        matrix = jnp.where(offset == tap_id, taps[tap_id], matrix)
    return matrix.astype(out_type)


def contract(form, left, right):
    if left.dtype == jnp.bfloat16:
        return jnp.einsum(form, left, right, preferred_element_type=jnp.float32)
    return jnp.einsum(form, left, right, precision=lax.Precision.HIGHEST)


def cut_along_rows(extended, count_out):
    matrix = band_matrix(extended.shape[1], count_out, extended.dtype)
    return contract("fic,io->foc", extended, matrix)


def cut_along_cols(extended, count_out):
    block_width = count_out // 4
    span_in = STRIDE * block_width + 2 * (TAPS // 2)
    matrix = band_matrix(span_in, block_width, extended.dtype)
    pieces = []
    for block_id in range(4):
        begin_at = STRIDE * block_width * block_id
        window = extended[:, :, begin_at : begin_at + span_in]
        pieces.append(contract("frc,co->fro", window, matrix))
    return jnp.concatenate(pieces, axis=2)


def weight_of(global_ids, length):
    return 0.5 - 0.5 * jnp.cos(2 * jnp.pi * global_ids.astype(jnp.float32) / length)


def angle_tables(point_ids, count_freq, length):
    freq_ids = lax.broadcasted_iota(jnp.int32, (point_ids.shape[0], count_freq), 1)
    reduced = point_ids[:, None] * freq_ids % length
    angles = 2 * jnp.pi / length * reduced.astype(jnp.float32)
    return (jnp.cos(angles), jnp.sin(angles))


def factor_of(length):
    factor_one = math.isqrt(length)
    while length % factor_one:
        factor_one = factor_one - 1
    return factor_one


def highest(form, left, right):
    return jnp.einsum(form, left, right, precision=lax.Precision.HIGHEST)


def dft_last(real_in, imag_in, length):
    factor_one = factor_of(length)
    factor_two = length // factor_one
    leading = real_in.shape[:-1]
    real_grid = real_in.reshape(leading + (factor_one, factor_two))
    cos_one, sin_one = angle_tables(jnp.arange(factor_one, dtype=jnp.int32), factor_one, factor_one)
    real_step = highest("...ab,ak->...kb", real_grid, cos_one)
    imag_step = -highest("...ab,ak->...kb", real_grid, sin_one)
    if imag_in is not None:
        imag_grid = imag_in.reshape(leading + (factor_one, factor_two))
        real_step = real_step + highest("...ab,ak->...kb", imag_grid, sin_one)
        imag_step = imag_step + highest("...ab,ak->...kb", imag_grid, cos_one)
    twiddle_cos, twiddle_sin = angle_tables(
        jnp.arange(factor_one, dtype=jnp.int32), factor_two, length
    )
    real_turned = real_step * twiddle_cos + imag_step * twiddle_sin
    imag_turned = imag_step * twiddle_cos - real_step * twiddle_sin
    cos_two, sin_two = angle_tables(jnp.arange(factor_two, dtype=jnp.int32), factor_two, factor_two)
    real_out = highest("...kb,bm->...mk", real_turned, cos_two) + highest(
        "...kb,bm->...mk", imag_turned, sin_two
    )
    imag_out = highest("...kb,bm->...mk", imag_turned, cos_two) - highest(
        "...kb,bm->...mk", real_turned, sin_two
    )
    return (real_out.reshape(leading + (length,)), imag_out.reshape(leading + (length,)))


def spread_kernel(src_ref, out_ref, got, filler, send_sem, recv_sem):
    devices = got.shape[0]
    cols = lax.axis_size("cols")
    me = lax.axis_index("rows") * cols + lax.axis_index("cols")
    barrier = pltpu.get_barrier_semaphore()

    def place(step):
        other = lax.rem(me + step, devices)
        return other, (other // cols, lax.rem(other, cols))

    @pl.loop(1, devices)
    def _(step):
        pl.semaphore_signal(
            barrier, inc=1, device_id=place(step)[1], device_id_type=pl.DeviceIdType.MESH
        )

    pl.semaphore_wait(barrier, devices - 1)

    @pl.loop(1, devices)
    def _(step):
        other, spot = place(step)
        pltpu.make_async_remote_copy(
            src_ref=src_ref.at[pl.ds(other, 1)],
            dst_ref=got.at[pl.ds(me, 1)],
            send_sem=send_sem,
            recv_sem=recv_sem,
            device_id=spot,
            device_id_type=pl.DeviceIdType.MESH,
        ).start()

    pltpu.make_async_copy(filler, filler, recv_sem).wait()
    pltpu.make_async_copy(filler, filler, send_sem).wait()
    got[pl.ds(me, 1)] = src_ref[pl.ds(me, 1)]
    out_ref[...] = got[...]


def spread(blocks):
    shape = blocks.shape
    return pl.pallas_call(
        spread_kernel,
        out_shape=jax.ShapeDtypeStruct(shape, jnp.float32),
        in_specs=[pl.BlockSpec(memory_space=pltpu.VMEM)],
        out_specs=pl.BlockSpec(memory_space=pltpu.VMEM),
        scratch_shapes=[
            pltpu.VMEM(shape, jnp.float32),
            pltpu.VMEM((shape[0] - 1,) + shape[1:], jnp.float32),
            pltpu.SemaphoreType.DMA,
            pltpu.SemaphoreType.DMA,
        ],
        compiler_params=pltpu.CompilerParams(collective_id=0, has_side_effects=True),
    )(blocks)


def local(field):
    tap_reach = TAPS // 2
    row_devices = lax.axis_size("rows")
    raw_rows = field.shape[1]
    raw_cols = field.shape[2]
    out_rows = raw_rows // STRIDE
    out_cols = raw_cols // STRIDE
    length = out_rows * row_devices
    half_length = length // 2
    extended = extended_2(field, (("rows", 1),), tap_reach)
    rowcut = cut_along_rows(extended, out_rows)
    widened = extended_2(rowcut, (("cols", 2),), tap_reach)
    cut = cut_along_cols(widened, out_cols)
    row_global = lax.axis_index("rows") * out_rows + jnp.arange(out_rows, dtype=jnp.int32)
    col_global = lax.axis_index("cols") * out_cols + jnp.arange(out_cols, dtype=jnp.int32)
    tapered = (
        cut
        * weight_of(row_global, length)[None, :, None]
        * weight_of(col_global, length)[None, None, :]
    )
    grouped = lax.all_to_all(tapered, "cols", split_axis=1, concat_axis=2, tiled=True)
    real_col, imag_col = dft_last(grouped, None, length)
    partial_value = jnp.stack([real_col[..., :half_length], imag_col[..., :half_length]], axis=1)
    partial_value = jnp.swapaxes(partial_value, 2, 3)
    devices = row_devices * lax.axis_size("cols")
    blocks = partial_value.reshape(2, devices, half_length // devices, -1)
    blocks = jnp.transpose(blocks, (1, 0, 2, 3)).reshape(devices, -1)
    size = blocks.shape[1]
    blocks = jnp.pad(blocks, ((0, 0), (0, -size % 128))).reshape(devices, -1, 128)
    arrived = spread(blocks).reshape(devices, -1)[:, :size]
    arrived = arrived.reshape(devices, 2, half_length // devices, -1)
    arrived = jnp.transpose(arrived, (1, 2, 0, 3)).reshape(1, 2, half_length // devices, length)
    real_row, imag_row = dft_last(arrived[:, 0], arrived[:, 1], length)
    return (real_row * real_row + imag_row * imag_row) * (8.0 / (length * length))


def solution(mesh):
    return jax.shard_map(
        local,
        mesh=mesh,
        in_specs=(P(None, "rows", "cols"),),
        out_specs=P(None, ("rows", "cols"), None),
        check_vma=False,
    )
```

```python
import jax
import jax.numpy as jnp
import ml_dtypes
import numpy as np
from jax import lax
from jax.experimental import pallas as pl
from jax.experimental.pallas import tpu as pltpu
from jax.sharding import PartitionSpec as P

TAPS = 33
STRIDE = 8
REACH = TAPS // 2
MESH = pl.DeviceIdType.MESH

ROWS, COLS = 32, 4
DEVICES = ROWS * COLS
LENGTH = 2304
RADIX = LENGTH // DEVICES
RAW_ROWS = LENGTH * STRIDE // ROWS
RAW_COLS = LENGTH * STRIDE // COLS
OUT_COLS = RAW_COLS // STRIDE
SLOT = 24
LANES = 128
WIDE = 5 * LANES
HALF = RADIX // 2


def taps_table():
    tap_ids = np.arange(TAPS, dtype=np.float32)
    shaped = np.sinc((tap_ids - np.float32(REACH)) / np.float32(STRIDE)).astype(np.float32)
    shaped = shaped * (
        np.float32(0.54)
        - np.float32(0.46) * np.cos(np.float32(2 * np.pi) * tap_ids / np.float32(TAPS - 1))
    )
    shaped = shaped / np.sum(shaped)
    return shaped.astype(ml_dtypes.bfloat16).astype(np.float32)


def tap_at(offset):
    taps = taps_table()
    inside = (offset >= 0) & (offset < TAPS)
    return np.where(inside, taps[np.clip(offset, 0, TAPS - 1)], 0).astype(ml_dtypes.bfloat16)


def split(matrix):
    high = matrix.astype(ml_dtypes.bfloat16)
    low = (matrix - high.astype(np.float64)).astype(ml_dtypes.bfloat16)
    return high, low


def tables():
    own = np.full((COLS, SLOT), -(10**6))
    own[:, :RADIX] = RADIX * np.arange(COLS)[:, None] + np.arange(RADIX)
    own[0, RADIX : RADIX + 2] = [-2, -1]
    own[-1, RADIX : RADIX + 2] = [COLS * RADIX, COLS * RADIX + 1]
    raw = np.arange(RAW_ROWS)
    row_band = tap_at(raw[None, :] - STRIDE * own.reshape(-1, 1) + REACH)

    lane = np.arange(LANES)
    inner = tap_at(np.arange(10 * LANES)[:, None] - LANES - STRIDE * lane[None, :] + REACH)
    edge = tap_at(lane[:, None] - STRIDE * (lane[None, :] - LANES) + REACH)
    col_band = np.concatenate([inner, edge], axis=0)

    angle = 2 * np.pi / LANES * (lane[:, None] * lane[None, :] % LANES)
    cos, sin = np.cos(angle), np.sin(angle)
    wave = np.block([[cos, -sin], [sin, cos]])
    first = np.concatenate([wave[:, : LANES // 2], wave[:, LANES : LANES + LANES // 2]], axis=1).T
    matrices = np.concatenate(split(first) + split(wave), axis=0)

    turn = 2 * np.pi / LENGTH * (np.arange(RADIX)[:, None] * lane[None, :])
    twiddles = np.stack([np.cos(turn), np.sin(turn)]).astype(np.float32)

    window = 0.5 - 0.5 * np.cos(2 * np.pi * np.arange(LENGTH) / LENGTH)
    row_window = np.zeros((DEVICES, SLOT))
    row_window[:, :RADIX] = window.reshape(DEVICES, RADIX)
    row_window = np.broadcast_to(row_window[:, :, None], (DEVICES, SLOT, LANES))
    col_window = np.broadcast_to(window[None, :], (8, LENGTH))
    return (
        row_band,
        col_band,
        matrices,
        twiddles,
        row_window.astype(np.float32),
        col_window.astype(np.float32),
    )


def real_nine(points):
    sums = [points[m] + points[9 - m] for m in range(1, 5)]
    gaps = [points[m] - points[9 - m] for m in range(1, 5)]
    reals, imags = [points[0] + sums[0] + sums[1] + sums[2] + sums[3]], [None]
    for freq in range(1, 5):
        real, imag = points[0], None
        for m in range(1, 5):
            phase = 2 * np.pi * (m * freq % 9) / 9
            real = real + sums[m - 1] * np.float32(np.cos(phase))
            term = gaps[m - 1] * np.float32(-np.sin(phase))
            imag = term if imag is None else imag + term
        reals.append(real)
        imags.append(imag)
    return reals, imags


def folded(points):
    evens = [points[2 * b % 18] for b in range(9)]
    odds = [points[(9 + 2 * b) % 18] for b in range(9)]
    return (
        real_nine([x + y for x, y in zip(evens, odds)]),
        real_nine([x - y for x, y in zip(evens, odds)]),
    )


def real_eighteen(points):
    both = folded(points)
    out = []
    for freq in range(18):
        reals, imags = both[freq % 2]
        at = freq % 9
        if at == 0:
            out.append((reals[0], None))
        elif at <= 4:
            out.append((reals[at], imags[at]))
        else:
            out.append((reals[9 - at], -imags[9 - at]))
    return out


def complex_eighteen(real_points, imag_points):
    both_real, both_imag = folded(real_points), folded(imag_points)
    out = []
    for freq in range(18):
        (a_re, a_im), (b_re, b_im) = both_real[freq % 2], both_imag[freq % 2]
        at = freq % 9
        if at == 0:
            out.append((a_re[0], b_re[0]))
        elif at <= 4:
            out.append((a_re[at] - b_im[at], a_im[at] + b_re[at]))
        else:
            out.append((a_re[9 - at] + b_im[9 - at], b_re[9 - at] - a_im[9 - at]))
    return out


def halves(value):
    high = value.astype(jnp.bfloat16)
    low = (value - high.astype(jnp.float32)).astype(jnp.bfloat16)
    return high, low


def product(left, right, dims):
    return lax.dot_general(left, right, (dims, ((), ())), preferred_element_type=jnp.float32)


def joined(blocks):
    lane = lax.broadcasted_iota(jnp.int32, (8, LANES), 1)
    turned = [pltpu.roll(b, 64, 1) if i % 2 else b for i, b in enumerate(blocks)]
    part = [[b[:, LANES * t : LANES * (t + 1)] for t in range(5)] for b in turned]
    zero = jnp.zeros((8, LANES), jnp.float32)
    out = part[0][:4]
    out.append(jnp.where(lane < 66, part[0][4], zero) + jnp.where(lane >= 62, part[1][0], zero))
    out += part[1][1:4]
    out.append(part[1][4] + jnp.where(lane >= 126, part[2][4], zero))
    out.append(part[2][0] + jnp.where(lane < 2, part[1][0], zero))
    out += part[2][1:4]
    out.append(jnp.where(lane < 66, part[2][4], zero) + jnp.where(lane >= 62, part[3][0], zero))
    out += part[3][1:5]
    return out


def kernel(
    field, row_band_in, col_band_in, matrices_in, twiddles_in, row_window_in, col_window_in,
    power,
    raw, row_band, col_band, matrices, twiddles, row_window, col_window,
    rowcut, cut, gathered, border, edges, turned, leaving, arrived, mixed, filler,
    load_sem, near_send, near_recv, edge_recv, far_send, far_recv,
):
    p, q = lax.axis_index("rows"), lax.axis_index("cols")
    me = p * COLS + q
    chunks = [(1024 * t, min(1024, RAW_COLS - 1024 * t)) for t in range(5)]
    loads = [
        pltpu.make_async_copy(row_band_in, row_band, load_sem.at[5]),
        pltpu.make_async_copy(col_band_in, col_band, load_sem.at[6]),
        pltpu.make_async_copy(matrices_in, matrices, load_sem.at[7]),
        pltpu.make_async_copy(twiddles_in, twiddles, load_sem.at[8]),
        pltpu.make_async_copy(row_window_in.at[me], row_window, load_sem.at[9]),
        pltpu.make_async_copy(col_window_in, col_window, load_sem.at[10]),
    ]
    field_loads = [
        pltpu.make_async_copy(
            field.at[0, :, pl.ds(begin, size)], raw.at[:, pl.ds(begin, size)], load_sem.at[t]
        )
        for t, (begin, size) in enumerate(chunks)
    ]
    for copy in loads[:1] + field_loads[:1] + loads[1:2] + field_loads[1:] + loads[2:]:
        copy.start()

    barrier = pltpu.get_barrier_semaphore()

    @pl.loop(1, DEVICES)
    def _(step):
        other = (me + step) & (DEVICES - 1)
        pl.semaphore_signal(
            barrier, inc=1, device_id=(other >> 2, other & 3), device_id_type=MESH
        )

    for row in (HALF * SLOT, 256 + HALF * SLOT):
        turned[pl.ds(row, 256 - HALF * SLOT), :] = jnp.zeros((256 - HALF * SLOT, 256), jnp.float32)
    edges[...] = jnp.zeros_like(edges)

    loads[0].wait()
    for t, (begin, size) in enumerate(chunks):
        field_loads[t].wait()
        if t == 1:
            loads[1].wait()
        part = product(row_band[...], raw[:, begin : begin + size], ((1,), (0,)))
        high, low = halves(part)
        rowcut[: COLS * SLOT, begin : begin + size] = high
        rowcut[COLS * SLOT :, begin : begin + size] = low
        blocks = [] if t == 0 else ([t - 1, t] if t == 4 else [t - 1])
        for u in blocks:
            lo, hi = max(1024 * u - LANES, 0), min(1024 * u + 1024 + LANES, RAW_COLS)
            skip = lo - (1024 * u - LANES)
            both = product(
                rowcut[:, lo:hi], col_band[skip : skip + hi - lo, :], ((1,), (0,))
            )
            if u == 4:
                both = both + product(
                    rowcut[:, :LANES], col_band[10 * LANES :, :], ((1,), (0,))
                )
            cut[:, LANES * u : LANES * (u + 1)] = both[: COLS * SLOT] + both[COLS * SLOT :]

    pl.semaphore_wait(barrier, DEVICES - 1)
    near = []
    for step in range(1, COLS):
        to = (q + step) & 3
        near.append(
            pltpu.make_async_remote_copy(
                src_ref=cut.at[pl.ds(pl.multiple_of(to * SLOT, 8), SLOT), :],
                dst_ref=gathered.at[q],
                send_sem=near_send.at[step - 1],
                recv_sem=near_recv.at[q],
                device_id=(p, to),
                device_id_type=MESH,
            )
        )
    for side, (row, to_p, to_q) in enumerate(
        ((3 * SLOT + 16, (p + 1) & 31, 3 * 0), (16, (p + 31) & 31, 3))
    ):
        near.append(
            pltpu.make_async_remote_copy(
                src_ref=cut.at[pl.ds(row, 8), :],
                dst_ref=border.at[q],
                send_sem=near_send.at[3 + side],
                recv_sem=edge_recv.at[q],
                device_id=(to_p, to_q),
                device_id_type=MESH,
            )
        )
    for copy in near:
        copy.start()
    gathered[q] = cut[pl.ds(pl.multiple_of(q * SLOT, 8), SLOT), :]
    for copy in loads[2:]:
        copy.wait()
    for step in range(1, COLS):
        source = (q + step) & 3
        pltpu.make_async_copy(
            gathered.at[source],
            gathered.at[source],
            near_recv.at[source],
        ).wait()

    row_id = lax.broadcasted_iota(jnp.int32, (8, LANES), 0)

    @pl.when((q == 0) | (q == 3))
    def _():
        for source in range(COLS):
            pltpu.make_async_copy(
                border.at[source], border.at[source], edge_recv.at[source]
            ).wait()
        valid = ((q == 0) & (p > 0)) | ((q == 3) & (p < ROWS - 1))
        keep = jnp.where(valid, 2, 0)
        for t, tile in enumerate(joined([border[source] for source in range(COLS)])):
            moved = pltpu.roll(tile, 6, 0)
            edges[:, LANES * t : LANES * (t + 1)] = jnp.where(row_id < keep, moved, 0.0)

    for s in range(3):
        rows = slice(8 * s, 8 * s + 8)
        points = joined([gathered[source, rows, :] for source in range(COLS)])
        if s == 2:
            points = [jnp.where(row_id < 2, x, 0.0) for x in points]
        if s != 1:
            flag = jnp.where(q == (0 if s == 0 else 3), 1.0, 0.0).astype(jnp.float32)
            points = [
                x + flag * edges[:, LANES * t : LANES * (t + 1)] for t, x in enumerate(points)
            ]
        points = [
            x * row_window[rows, :] * col_window[:, LANES * t : LANES * (t + 1)]
            for t, x in enumerate(points)
        ]
        for freq, (real, imag) in enumerate(real_eighteen(points)):
            at = (freq // HALF) * 256 + (freq % HALF) * SLOT + 8 * s
            cos, sin = twiddles[0, freq : freq + 1, :], twiddles[1, freq : freq + 1, :]
            if imag is None:
                turned[at : at + 8, :LANES] = real * cos
                turned[at : at + 8, LANES:] = -real * sin
            else:
                turned[at : at + 8, :LANES] = real * cos + imag * sin
                turned[at : at + 8, LANES:] = imag * cos - real * sin

    first_high, first_low = matrices[:LANES, :], matrices[LANES : 2 * LANES, :]
    for h in range(2):
        high, low = halves(turned[256 * h : 256 * (h + 1), :])
        both = (
            product(first_high, low, ((1,), (1,)))
            + product(first_low, high, ((1,), (1,)))
            + product(first_high, high, ((1,), (1,)))
        )
        leaving[0, :, 256 * h : 256 * (h + 1)] = both[: LANES // 2]
        leaving[1, :, 256 * h : 256 * (h + 1)] = both[LANES // 2 :]

    def block_of(other):
        lanes = pl.multiple_of((other & 1) * 256, 256)
        return leaving.at[:, pl.ds(other >> 1, 1), pl.ds(lanes, 256)]

    @pl.loop(1, DEVICES)
    def _(step):
        other = (me + step) & (DEVICES - 1)
        pltpu.make_async_remote_copy(
            src_ref=block_of(other),
            dst_ref=arrived.at[:, pl.ds(me, 1), :],
            send_sem=far_send,
            recv_sem=far_recv,
            device_id=(other >> 2, other & 3),
            device_id_type=MESH,
        ).start()

    pltpu.make_async_copy(block_of(me), arrived.at[:, pl.ds(me, 1), :], far_recv).start()
    pltpu.make_async_copy(arrived, arrived, far_recv).wait()

    wave_high, wave_low = matrices[2 * LANES : 4 * LANES, :], matrices[4 * LANES :, :]
    high, low = halves(arrived[...].reshape(2 * DEVICES, 256).T)
    both = (
        product(low, wave_high, ((1,), (0,)))
        + product(high, wave_low, ((1,), (0,)))
        + product(high, wave_high, ((1,), (0,)))
    )
    mixed[0], mixed[1] = both[:, :LANES], both[:, LANES:]
    real_points, imag_points = [], []
    for r in range(RADIX):
        real = mixed[0, pl.ds(r, HALF, stride=SLOT), :]
        imag = mixed[1, pl.ds(r, HALF, stride=SLOT), :]
        cos, sin = twiddles[0, r : r + 1, :], twiddles[1, r : r + 1, :]
        real_points.append(real * cos + imag * sin)
        imag_points.append(imag * cos - real * sin)
    for freq, (real, imag) in enumerate(complex_eighteen(real_points, imag_points)):
        power[:, LANES * freq : LANES * (freq + 1)] = (real * real + imag * imag) * np.float32(
            8.0 / (LENGTH * LENGTH)
        )

    for copy in near:
        copy.wait_send()
    pltpu.make_async_copy(filler, filler, far_send).wait()


def local(field):
    constants = tables()
    anywhere = pl.BlockSpec(memory_space=pltpu.HBM)
    f32, bf16 = jnp.float32, jnp.bfloat16
    power = pl.pallas_call(
        kernel,
        out_shape=jax.ShapeDtypeStruct((HALF, LENGTH), f32),
        in_specs=[anywhere] * (1 + len(constants)),
        out_specs=pl.BlockSpec(memory_space=pltpu.VMEM),
        scratch_shapes=[
            pltpu.VMEM((RAW_ROWS, RAW_COLS), bf16),
            pltpu.VMEM(constants[0].shape, bf16),
            pltpu.VMEM(constants[1].shape, bf16),
            pltpu.VMEM(constants[2].shape, bf16),
            pltpu.VMEM(constants[3].shape, f32),
            pltpu.VMEM((SLOT, LANES), f32),
            pltpu.VMEM(constants[5].shape, f32),
            pltpu.VMEM((2 * COLS * SLOT, RAW_COLS), bf16),
            pltpu.VMEM((COLS * SLOT, WIDE), f32),
            pltpu.VMEM((COLS, SLOT, WIDE), f32),
            pltpu.VMEM((COLS, 8, WIDE), f32),
            pltpu.VMEM((8, LENGTH), f32),
            pltpu.VMEM((512, 256), f32),
            pltpu.VMEM((2, LANES // 2, 512), f32),
            pltpu.VMEM((2, DEVICES, 256), f32),
            pltpu.VMEM((2, 256, LANES), f32),
            pltpu.VMEM((DEVICES - 1, 4, LANES), f32),
            pltpu.SemaphoreType.DMA((11,)),
            pltpu.SemaphoreType.DMA((5,)),
            pltpu.SemaphoreType.DMA((COLS,)),
            pltpu.SemaphoreType.DMA((COLS,)),
            pltpu.SemaphoreType.DMA,
            pltpu.SemaphoreType.DMA,
        ],
        compiler_params=pltpu.CompilerParams(
            collective_id=0, has_side_effects=True, vmem_limit_bytes=48 * 2**20
        ),
    )(field, *[jnp.asarray(c) for c in constants])
    return power[None]


def solution(mesh):
    return jax.shard_map(
        local,
        mesh=mesh,
        in_specs=(P(None, "rows", "cols"),),
        out_specs=P(None, ("rows", "cols"), None),
        check_vma=False,
    )
```

```python
import jax
import jax.numpy as jnp
import ml_dtypes
import numpy as np
from jax import lax
from jax.experimental import pallas as pl
from jax.experimental.pallas import tpu as pltpu
from jax.sharding import PartitionSpec as P

TAPS = 33
STRIDE = 8
REACH = TAPS // 2
MESH = pl.DeviceIdType.MESH

ROWS, COLS = 32, 4
DEVICES = ROWS * COLS
LENGTH = 2304
RADIX = LENGTH // DEVICES
RAW_ROWS = LENGTH * STRIDE // ROWS
RAW_COLS = LENGTH * STRIDE // COLS
OUT_COLS = RAW_COLS // STRIDE
SLOT = 24
LANES = 128
WIDE = 5 * LANES
HALF = RADIX // 2


def taps_table():
    tap_ids = np.arange(TAPS, dtype=np.float32)
    shaped = np.sinc((tap_ids - np.float32(REACH)) / np.float32(STRIDE)).astype(np.float32)
    shaped = shaped * (
        np.float32(0.54)
        - np.float32(0.46) * np.cos(np.float32(2 * np.pi) * tap_ids / np.float32(TAPS - 1))
    )
    shaped = shaped / np.sum(shaped)
    return shaped.astype(ml_dtypes.bfloat16).astype(np.float32)


def tap_at(offset):
    taps = taps_table()
    inside = (offset >= 0) & (offset < TAPS)
    return np.where(inside, taps[np.clip(offset, 0, TAPS - 1)], 0).astype(ml_dtypes.bfloat16)


def split(matrix):
    high = matrix.astype(ml_dtypes.bfloat16)
    low = (matrix - high.astype(np.float64)).astype(ml_dtypes.bfloat16)
    return high, low


def tables():
    own = np.full((COLS, SLOT), -(10**6))
    own[:, :RADIX] = RADIX * np.arange(COLS)[:, None] + np.arange(RADIX)
    own[0, RADIX : RADIX + 2] = [-2, -1]
    own[-1, RADIX : RADIX + 2] = [COLS * RADIX, COLS * RADIX + 1]
    raw = np.arange(RAW_ROWS)
    row_band = tap_at(raw[None, :] - STRIDE * own.reshape(-1, 1) + REACH)

    lane = np.arange(LANES)
    inner = tap_at(np.arange(10 * LANES)[:, None] - LANES - STRIDE * lane[None, :] + REACH)
    edge = tap_at(lane[:, None] - STRIDE * (lane[None, :] - LANES) + REACH)
    col_band = np.concatenate([inner, edge], axis=0)

    angle = 2 * np.pi / LANES * (lane[:, None] * lane[None, :] % LANES)
    cos, sin = np.cos(angle), np.sin(angle)
    wave = np.block([[cos, -sin], [sin, cos]])
    first = np.concatenate([wave[:, : LANES // 2], wave[:, LANES : LANES + LANES // 2]], axis=1).T
    matrices = np.concatenate(split(first) + split(wave), axis=0)

    turn = 2 * np.pi / LENGTH * (np.arange(RADIX)[:, None] * lane[None, :])
    twiddles = np.stack([np.cos(turn), np.sin(turn)]).astype(np.float32)

    window = 0.5 - 0.5 * np.cos(2 * np.pi * np.arange(LENGTH) / LENGTH)
    row_window = np.zeros((DEVICES, SLOT))
    row_window[:, :RADIX] = window.reshape(DEVICES, RADIX)
    row_window = np.broadcast_to(row_window[:, :, None], (DEVICES, SLOT, LANES))
    col_window = np.broadcast_to(window[None, :], (8, LENGTH))
    return (
        row_band,
        col_band,
        matrices,
        twiddles,
        row_window.astype(np.float32),
        col_window.astype(np.float32),
    )


def real_nine(points):
    sums = [points[m] + points[9 - m] for m in range(1, 5)]
    gaps = [points[m] - points[9 - m] for m in range(1, 5)]
    reals, imags = [points[0] + sums[0] + sums[1] + sums[2] + sums[3]], [None]
    for freq in range(1, 5):
        real, imag = points[0], None
        for m in range(1, 5):
            phase = 2 * np.pi * (m * freq % 9) / 9
            real = real + sums[m - 1] * np.float32(np.cos(phase))
            term = gaps[m - 1] * np.float32(-np.sin(phase))
            imag = term if imag is None else imag + term
        reals.append(real)
        imags.append(imag)
    return reals, imags


def folded(points):
    evens = [points[2 * b % 18] for b in range(9)]
    odds = [points[(9 + 2 * b) % 18] for b in range(9)]
    return (
        real_nine([x + y for x, y in zip(evens, odds)]),
        real_nine([x - y for x, y in zip(evens, odds)]),
    )


def real_eighteen(points):
    both = folded(points)
    out = []
    for freq in range(18):
        reals, imags = both[freq % 2]
        at = freq % 9
        if at == 0:
            out.append((reals[0], None))
        elif at <= 4:
            out.append((reals[at], imags[at]))
        else:
            out.append((reals[9 - at], -imags[9 - at]))
    return out


def complex_eighteen(real_points, imag_points):
    both_real, both_imag = folded(real_points), folded(imag_points)
    out = []
    for freq in range(18):
        (a_re, a_im), (b_re, b_im) = both_real[freq % 2], both_imag[freq % 2]
        at = freq % 9
        if at == 0:
            out.append((a_re[0], b_re[0]))
        elif at <= 4:
            out.append((a_re[at] - b_im[at], a_im[at] + b_re[at]))
        else:
            out.append((a_re[9 - at] + b_im[9 - at], b_re[9 - at] - a_im[9 - at]))
    return out


def halves(value):
    high = value.astype(jnp.bfloat16)
    low = (value - high.astype(jnp.float32)).astype(jnp.bfloat16)
    return high, low


def product(left, right, dims):
    return lax.dot_general(left, right, (dims, ((), ())), preferred_element_type=jnp.float32)


def joined(blocks):
    lane = lax.broadcasted_iota(jnp.int32, (8, LANES), 1)
    turned = [pltpu.roll(b, 64, 1) if i % 2 else b for i, b in enumerate(blocks)]
    part = [[b[:, LANES * t : LANES * (t + 1)] for t in range(5)] for b in turned]
    zero = jnp.zeros((8, LANES), jnp.float32)
    out = part[0][:4]
    out.append(jnp.where(lane < 66, part[0][4], zero) + jnp.where(lane >= 62, part[1][0], zero))
    out += part[1][1:4]
    out.append(part[1][4] + jnp.where(lane >= 126, part[2][4], zero))
    out.append(part[2][0] + jnp.where(lane < 2, part[1][0], zero))
    out += part[2][1:4]
    out.append(jnp.where(lane < 66, part[2][4], zero) + jnp.where(lane >= 62, part[3][0], zero))
    out += part[3][1:5]
    return out


def kernel(
    field, row_band_in, col_band_in, matrices_in, twiddles_in, row_window_in, col_window_in,
    power,
    raw, row_band, col_band, matrices, twiddles, row_window, col_window,
    rowcut, cut, gathered, border, edges, turned, leaving, arrived, mixed, filler,
    load_sem, near_send, near_recv, edge_recv, far_send, far_recv,
):
    p, q = lax.axis_index("rows"), lax.axis_index("cols")
    me = p * COLS + q
    chunks = [(1024 * t, min(1024, RAW_COLS - 1024 * t)) for t in range(5)]
    loads = [
        pltpu.make_async_copy(row_band_in, row_band, load_sem.at[5]),
        pltpu.make_async_copy(col_band_in, col_band, load_sem.at[6]),
        pltpu.make_async_copy(matrices_in, matrices, load_sem.at[7]),
        pltpu.make_async_copy(twiddles_in, twiddles, load_sem.at[8]),
        pltpu.make_async_copy(row_window_in.at[me], row_window, load_sem.at[9]),
        pltpu.make_async_copy(col_window_in, col_window, load_sem.at[10]),
    ]
    field_loads = [
        pltpu.make_async_copy(
            field.at[0, :, pl.ds(begin, size)], raw.at[:, pl.ds(begin, size)], load_sem.at[t]
        )
        for t, (begin, size) in enumerate(chunks)
    ]
    for copy in loads[:1] + field_loads[:1] + loads[1:2] + field_loads[1:] + loads[2:]:
        copy.start()

    barrier = pltpu.get_barrier_semaphore()

    @pl.loop(1, DEVICES)
    def _(step):
        other = (me + step) & (DEVICES - 1)
        pl.semaphore_signal(
            barrier, inc=1, device_id=(other >> 2, other & 3), device_id_type=MESH
        )

    for row in (HALF * SLOT, 256 + HALF * SLOT):
        turned[pl.ds(row, 256 - HALF * SLOT), :] = jnp.zeros((256 - HALF * SLOT, 256), jnp.float32)
    edges[...] = jnp.zeros_like(edges)

    loads[0].wait()
    for t, (begin, size) in enumerate(chunks):
        field_loads[t].wait()
        if t == 1:
            loads[1].wait()
        part = product(row_band[...], raw[:, begin : begin + size], ((1,), (0,)))
        high, low = halves(part)
        rowcut[: COLS * SLOT, begin : begin + size] = high
        rowcut[COLS * SLOT :, begin : begin + size] = low
        blocks = [] if t == 0 else ([t - 1, t] if t == 4 else [t - 1])
        for u in blocks:
            lo, hi = max(1024 * u - LANES, 0), min(1024 * u + 1024 + LANES, RAW_COLS)
            skip = lo - (1024 * u - LANES)
            both = product(
                rowcut[:, lo:hi], col_band[skip : skip + hi - lo, :], ((1,), (0,))
            )
            if u == 4:
                both = both + product(
                    rowcut[:, :LANES], col_band[10 * LANES :, :], ((1,), (0,))
                )
            cut[:, LANES * u : LANES * (u + 1)] = both[: COLS * SLOT] + both[COLS * SLOT :]

    pl.semaphore_wait(barrier, DEVICES - 1)
    near = []
    for step in range(1, COLS):
        to = (q + step) & 3
        near.append(
            pltpu.make_async_remote_copy(
                src_ref=cut.at[pl.ds(pl.multiple_of(to * SLOT, 8), SLOT), :],
                dst_ref=gathered.at[q],
                send_sem=near_send.at[step - 1],
                recv_sem=near_recv.at[q],
                device_id=(p, to),
                device_id_type=MESH,
            )
        )
    for side, (row, to_p, to_q) in enumerate(
        ((3 * SLOT + 16, (p + 1) & 31, 3 * 0), (16, (p + 31) & 31, 3))
    ):
        near.append(
            pltpu.make_async_remote_copy(
                src_ref=cut.at[pl.ds(row, 8), :],
                dst_ref=border.at[q],
                send_sem=near_send.at[3 + side],
                recv_sem=edge_recv.at[q],
                device_id=(to_p, to_q),
                device_id_type=MESH,
            )
        )
    for copy in near:
        copy.start()
    gathered[q] = cut[pl.ds(pl.multiple_of(q * SLOT, 8), SLOT), :]
    for copy in loads[2:]:
        copy.wait()
    for step in range(1, COLS):
        source = (q + step) & 3
        pltpu.make_async_copy(
            gathered.at[source],
            gathered.at[source],
            near_recv.at[source],
        ).wait()

    row_id = lax.broadcasted_iota(jnp.int32, (8, LANES), 0)

    @pl.when((q == 0) | (q == 3))
    def _():
        for source in range(COLS):
            pltpu.make_async_copy(
                border.at[source], border.at[source], edge_recv.at[source]
            ).wait()
        valid = ((q == 0) & (p > 0)) | ((q == 3) & (p < ROWS - 1))
        keep = jnp.where(valid, 2, 0)
        for t, tile in enumerate(joined([border[source] for source in range(COLS)])):
            moved = pltpu.roll(tile, 6, 0)
            edges[:, LANES * t : LANES * (t + 1)] = jnp.where(row_id < keep, moved, 0.0)

    for s in range(3):
        rows = slice(8 * s, 8 * s + 8)
        points = joined([gathered[source, rows, :] for source in range(COLS)])
        if s == 2:
            points = [jnp.where(row_id < 2, x, 0.0) for x in points]
        if s != 1:
            flag = jnp.where(q == (0 if s == 0 else 3), 1.0, 0.0).astype(jnp.float32)
            points = [
                x + flag * edges[:, LANES * t : LANES * (t + 1)] for t, x in enumerate(points)
            ]
        points = [
            x * row_window[rows, :] * col_window[:, LANES * t : LANES * (t + 1)]
            for t, x in enumerate(points)
        ]
        for freq, (real, imag) in enumerate(real_eighteen(points)):
            at = (freq // HALF) * 256 + (freq % HALF) * SLOT + 8 * s
            cos, sin = twiddles[0, freq : freq + 1, :], twiddles[1, freq : freq + 1, :]
            if imag is None:
                turned[at : at + 8, :LANES] = real * cos
                turned[at : at + 8, LANES:] = -real * sin
            else:
                turned[at : at + 8, :LANES] = real * cos + imag * sin
                turned[at : at + 8, LANES:] = imag * cos - real * sin

    first_high, first_low = matrices[:LANES, :], matrices[LANES : 2 * LANES, :]
    for h in range(2):
        high, low = halves(turned[256 * h : 256 * (h + 1), :])
        both = (
            product(first_high, low, ((1,), (1,)))
            + product(first_low, high, ((1,), (1,)))
            + product(first_high, high, ((1,), (1,)))
        )
        leaving[0, :, 256 * h : 256 * (h + 1)] = both[: LANES // 2]
        leaving[1, :, 256 * h : 256 * (h + 1)] = both[LANES // 2 :]

    def block_of(other):
        lanes = pl.multiple_of((other & 1) * 256, 256)
        return leaving.at[:, pl.ds(other >> 1, 1), pl.ds(lanes, 256)]

    @pl.loop(1, DEVICES)
    def _(step):
        other = (me + step) & (DEVICES - 1)
        pltpu.make_async_remote_copy(
            src_ref=block_of(other),
            dst_ref=arrived.at[:, pl.ds(me, 1), :],
            send_sem=far_send,
            recv_sem=far_recv,
            device_id=(other >> 2, other & 3),
            device_id_type=MESH,
        ).start()

    pltpu.make_async_copy(block_of(me), arrived.at[:, pl.ds(me, 1), :], far_recv).start()
    pltpu.make_async_copy(arrived, arrived, far_recv).wait()

    wave_high, wave_low = matrices[2 * LANES : 4 * LANES, :], matrices[4 * LANES :, :]
    high, low = halves(arrived[...].reshape(2 * DEVICES, 256).T)
    both = (
        product(low, wave_high, ((1,), (0,)))
        + product(high, wave_low, ((1,), (0,)))
        + product(high, wave_high, ((1,), (0,)))
    )
    mixed[0], mixed[1] = both[:, :LANES], both[:, LANES:]
    real_points, imag_points = [], []
    for r in range(RADIX):
        real = mixed[0, pl.ds(r, HALF, stride=SLOT), :]
        imag = mixed[1, pl.ds(r, HALF, stride=SLOT), :]
        cos, sin = twiddles[0, r : r + 1, :], twiddles[1, r : r + 1, :]
        real_points.append(real * cos + imag * sin)
        imag_points.append(imag * cos - real * sin)
    for freq, (real, imag) in enumerate(complex_eighteen(real_points, imag_points)):
        power[:, LANES * freq : LANES * (freq + 1)] = (real * real + imag * imag) * np.float32(
            8.0 / (LENGTH * LENGTH)
        )

    for copy in near:
        copy.wait_send()
    pltpu.make_async_copy(filler, filler, far_send).wait()


def local(field):
    constants = tables()
    anywhere = pl.BlockSpec(memory_space=pltpu.HBM)
    f32, bf16 = jnp.float32, jnp.bfloat16
    power = pl.pallas_call(
        kernel,
        out_shape=jax.ShapeDtypeStruct((HALF, LENGTH), f32),
        in_specs=[anywhere] * (1 + len(constants)),
        out_specs=pl.BlockSpec(memory_space=pltpu.VMEM),
        scratch_shapes=[
            pltpu.VMEM((RAW_ROWS, RAW_COLS), bf16),
            pltpu.VMEM(constants[0].shape, bf16),
            pltpu.VMEM(constants[1].shape, bf16),
            pltpu.VMEM(constants[2].shape, bf16),
            pltpu.VMEM(constants[3].shape, f32),
            pltpu.VMEM((SLOT, LANES), f32),
            pltpu.VMEM(constants[5].shape, f32),
            pltpu.VMEM((2 * COLS * SLOT, RAW_COLS), bf16),
            pltpu.VMEM((COLS * SLOT, WIDE), f32),
            pltpu.VMEM((COLS, SLOT, WIDE), f32),
            pltpu.VMEM((COLS, 8, WIDE), f32),
            pltpu.VMEM((8, LENGTH), f32),
            pltpu.VMEM((512, 256), f32),
            pltpu.VMEM((2, LANES // 2, 512), f32),
            pltpu.VMEM((2, DEVICES, 256), f32),
            pltpu.VMEM((2, 256, LANES), f32),
            pltpu.VMEM((DEVICES - 1, 4, LANES), f32),
            pltpu.SemaphoreType.DMA((11,)),
            pltpu.SemaphoreType.DMA((5,)),
            pltpu.SemaphoreType.DMA((COLS,)),
            pltpu.SemaphoreType.DMA((COLS,)),
            pltpu.SemaphoreType.DMA,
            pltpu.SemaphoreType.DMA,
        ],
        compiler_params=pltpu.CompilerParams(
            collective_id=0, has_side_effects=True, vmem_limit_bytes=56 * 2**20
        ),
    )(field, *[jnp.asarray(c) for c in constants])
    return power[None]


def solution(mesh):
    return jax.shard_map(
        local,
        mesh=mesh,
        in_specs=(P(None, "rows", "cols"),),
        out_specs=P(None, ("rows", "cols"), None),
        check_vma=False,
    )
```

```python
import jax
import jax.numpy as jnp
import ml_dtypes
import numpy as np
from jax import lax
from jax.experimental import pallas as pl
from jax.experimental.pallas import tpu as pltpu
from jax.sharding import PartitionSpec as P

TAPS = 33
STRIDE = 8
REACH = TAPS // 2
MESH = pl.DeviceIdType.MESH

ROWS, COLS = 32, 4
DEVICES = ROWS * COLS
LENGTH = 2304
RADIX = LENGTH // DEVICES
RAW_ROWS = LENGTH * STRIDE // ROWS
RAW_COLS = LENGTH * STRIDE // COLS
OUT_COLS = RAW_COLS // STRIDE
SLOT = 24
LANES = 128
WIDE = 5 * LANES
HALF = RADIX // 2


FARTHEST = 74
GROUP_A = [1, 2, 3]
GROUP_B = [4 * k for k in range(1, 8)]
GROUP_C = [32, 64, 96]
CUTS = [0, 640] + [640 + 512 * t for t in range(1, 8)] + [RAW_COLS]
CHUNKS = list(zip(CUTS[:-1], CUTS[1:]))


def taps_table():
    tap_ids = np.arange(TAPS, dtype=np.float32)
    shaped = np.sinc((tap_ids - np.float32(REACH)) / np.float32(STRIDE)).astype(np.float32)
    shaped = shaped * (
        np.float32(0.54)
        - np.float32(0.46) * np.cos(np.float32(2 * np.pi) * tap_ids / np.float32(TAPS - 1))
    )
    shaped = shaped / np.sum(shaped)
    return shaped.astype(ml_dtypes.bfloat16).astype(np.float32)


def tap_at(offset):
    taps = taps_table()
    inside = (offset >= 0) & (offset < TAPS)
    return np.where(inside, taps[np.clip(offset, 0, TAPS - 1)], 0).astype(ml_dtypes.bfloat16)


def split(matrix):
    high = matrix.astype(ml_dtypes.bfloat16)
    low = (matrix - high.astype(np.float64)).astype(ml_dtypes.bfloat16)
    return high, low


def tables():
    own = np.full((COLS, SLOT), -(10**6))
    own[:, :RADIX] = RADIX * np.arange(COLS)[:, None] + np.arange(RADIX)
    own[0, RADIX : RADIX + 2] = [-2, -1]
    own[-1, RADIX : RADIX + 2] = [COLS * RADIX, COLS * RADIX + 1]
    raw = np.arange(RAW_ROWS)
    row_band = tap_at(raw[None, :] - STRIDE * own.reshape(-1, 1) + REACH)

    lane = np.arange(LANES)
    inner = tap_at(np.arange(10 * LANES)[:, None] - LANES - STRIDE * lane[None, :] + REACH)
    edge = tap_at(lane[:, None] - STRIDE * (lane[None, :] - LANES) + REACH)
    col_band = np.concatenate([inner, edge], axis=0)

    angle = 2 * np.pi / LANES * (lane[:, None] * lane[None, :] % LANES)
    cos, sin = np.cos(angle), np.sin(angle)
    wave = np.block([[cos, -sin], [sin, cos]])
    first = np.concatenate([wave[:, : LANES // 2], wave[:, LANES : LANES + LANES // 2]], axis=1).T
    matrices = np.concatenate(split(first) + split(wave), axis=0)

    turn = 2 * np.pi / LENGTH * (np.arange(RADIX)[:, None] * lane[None, :])
    twiddles = np.stack([np.cos(turn), np.sin(turn)]).astype(np.float32)

    window = 0.5 - 0.5 * np.cos(2 * np.pi * np.arange(LENGTH) / LENGTH)
    row_window = np.zeros((DEVICES, SLOT))
    row_window[:, :RADIX] = window.reshape(DEVICES, RADIX)
    row_window = np.broadcast_to(row_window[:, :, None], (DEVICES, SLOT, LANES))
    col_window = np.broadcast_to(window.reshape(RADIX, 1, LANES), (RADIX, 8, LANES))
    twiddles = np.pad(twiddles, ((0, 0), (0, SLOT - RADIX), (0, 0)))
    floats = np.concatenate([row_window, twiddles, col_window.reshape(-1, SLOT, LANES)], axis=0)
    row_band = np.pad(row_band, ((0, COLS * SLOT), (0, WIDE - RAW_ROWS)))
    return row_band, col_band, matrices, floats.astype(np.float32)


def real_nine(points):
    sums = [points[m] + points[9 - m] for m in range(1, 5)]
    gaps = [points[m] - points[9 - m] for m in range(1, 5)]
    reals, imags = [points[0] + sums[0] + sums[1] + sums[2] + sums[3]], [None]
    for freq in range(1, 5):
        real, imag = points[0], None
        for m in range(1, 5):
            phase = 2 * np.pi * (m * freq % 9) / 9
            real = real + sums[m - 1] * np.float32(np.cos(phase))
            term = gaps[m - 1] * np.float32(-np.sin(phase))
            imag = term if imag is None else imag + term
        reals.append(real)
        imags.append(imag)
    return reals, imags


def folded(points):
    evens = [points[2 * b % 18] for b in range(9)]
    odds = [points[(9 + 2 * b) % 18] for b in range(9)]
    return (
        real_nine([x + y for x, y in zip(evens, odds)]),
        real_nine([x - y for x, y in zip(evens, odds)]),
    )


def real_eighteen(points):
    both = folded(points)
    out = []
    for freq in range(18):
        reals, imags = both[freq % 2]
        at = freq % 9
        if at == 0:
            out.append((reals[0], None))
        elif at <= 4:
            out.append((reals[at], imags[at]))
        else:
            out.append((reals[9 - at], -imags[9 - at]))
    return out


def complex_eighteen(real_points, imag_points):
    both_real, both_imag = folded(real_points), folded(imag_points)
    out = []
    for freq in range(18):
        (a_re, a_im), (b_re, b_im) = both_real[freq % 2], both_imag[freq % 2]
        at = freq % 9
        if at == 0:
            out.append((a_re[0], b_re[0]))
        elif at <= 4:
            out.append((a_re[at] - b_im[at], a_im[at] + b_re[at]))
        else:
            out.append((a_re[9 - at] + b_im[9 - at], b_re[9 - at] - a_im[9 - at]))
    return out


def halves(value):
    high = value.astype(jnp.bfloat16)
    low = (value - high.astype(jnp.float32)).astype(jnp.bfloat16)
    return high, low


def product(left, right, dims):
    return lax.dot_general(left, right, (dims, ((), ())), preferred_element_type=jnp.float32)


def joined(blocks):
    lane = lax.broadcasted_iota(jnp.int32, (8, LANES), 1)
    turned = [pltpu.roll(b, 64, 1) if i % 2 else b for i, b in enumerate(blocks)]
    part = [[b[:, LANES * t : LANES * (t + 1)] for t in range(5)] for b in turned]
    zero = jnp.zeros((8, LANES), jnp.float32)
    out = part[0][:4]
    out.append(jnp.where(lane < 66, part[0][4], zero) + jnp.where(lane >= 62, part[1][0], zero))
    out += part[1][1:4]
    out.append(part[1][4] + jnp.where(lane >= 126, part[2][4], zero))
    out.append(part[2][0] + jnp.where(lane < 2, part[1][0], zero))
    out += part[2][1:4]
    out.append(jnp.where(lane < 66, part[2][4], zero) + jnp.where(lane >= 62, part[3][0], zero))
    out += part[3][1:5]
    return out


def kernel(
    field, row_band_in, col_band_in, matrices_in, floats_in,
    power,
    raw, row_band, col_band, matrices, common, row_window,
    rowcut, cut, gathered, border, edges, turned, leaving, arrived, mixed, filler,
    load_sem, near_send, near_recv, edge_send, edge_recv, far_send, far_recv, group_ready, all_ready,
):
    p, q = lax.axis_index("rows"), lax.axis_index("cols")
    me = p * COLS + q
    def peer(k):
        return (p ^ (k >> 2), q ^ (k & 3))

    small = len(CHUNKS)
    loads = [
        pltpu.make_async_copy(row_band_in.at[pl.ds(0, COLS * SLOT)], row_band, load_sem.at[small]),
        pltpu.make_async_copy(col_band_in, col_band, load_sem.at[small + 1]),
        pltpu.make_async_copy(matrices_in, matrices, load_sem.at[small + 2]),
        pltpu.make_async_copy(floats_in.at[me], row_window, load_sem.at[small + 3]),
        pltpu.make_async_copy(
            floats_in.at[pl.ds(DEVICES, 2 + RADIX // 3)], common, load_sem.at[small + 4]
        ),
    ]
    field_loads = [
        pltpu.make_async_copy(
            field.at[0, :, pl.ds(lo, hi - lo)], raw.at[:, pl.ds(lo, hi - lo)], load_sem.at[t]
        )
        for t, (lo, hi) in enumerate(CHUNKS)
    ]
    for copy in loads[:1] + field_loads[:2] + loads[1:2]:
        copy.start()

    def signal(semaphore, device):
        pl.semaphore_signal(semaphore, inc=1, device_id=device, device_id_type=MESH)

    barrier = pltpu.get_barrier_semaphore()
    for k in GROUP_C + GROUP_B + GROUP_A:
        signal(barrier, peer(k))
    for side, to_p in ((0, (p + 31) & 31), (3, (p + 1) & 31)):

        @pl.when(q == side)
        def _():
            for to_q in range(COLS):
                signal(barrier, (to_p, to_q))

    for copy in field_loads[2:] + loads[2:]:
        copy.start()

    for row in (HALF * SLOT, 256 + HALF * SLOT):
        turned[pl.ds(row, 256 - HALF * SLOT), :] = jnp.zeros((256 - HALF * SLOT, 256), jnp.float32)
    edges[...] = jnp.zeros_like(edges)

    def row_copy(step, part, lo, size):
        to = (q + step) & 3
        return pltpu.make_async_remote_copy(
            src_ref=cut.at[pl.ds(pl.multiple_of(to * SLOT, 8), SLOT), pl.ds(lo, size)],
            dst_ref=gathered.at[q, :, pl.ds(lo, size)],
            send_sem=near_send.at[step, part],
            recv_sem=near_recv.at[q, part],
            device_id=(p, to),
            device_id_type=MESH,
        )

    def edge_copy(side, row):
        return pltpu.make_async_remote_copy(
            src_ref=cut.at[pl.ds((3 * SLOT, 0)[side] + RADIX + row, 1), :],
            dst_ref=border.at[q, pl.ds(row, 1), :],
            send_sem=edge_send.at[side, row],
            recv_sem=edge_recv.at[q, row],
            device_id=(((p + 1) & 31, 3 * 0), ((p + 31) & 31, 3))[side],
            device_id_type=MESH,
        )

    early = [row_copy(step, 0, 0, 4 * LANES) for step in (2, 1, 3)]
    late = [row_copy(step, 1, 4 * LANES, LANES) for step in (2, 1, 3)]
    late += [edge_copy(side, row) for side in range(2) for row in range(2)]

    loads[0].wait()
    for t, (begin, end) in enumerate(CHUNKS):
        field_loads[t].wait()
        part = product(row_band[:, :RAW_ROWS], raw[:, begin:end], ((1,), (0,)))
        high, low = halves(part)
        rowcut[: COLS * SLOT, begin:end] = high
        rowcut[COLS * SLOT :, begin:end] = low
        for u in range(5):
            if min(1024 * u + 1024 + LANES, RAW_COLS) != end:
                continue
            if u == 0:
                loads[1].wait()
            lo = max(1024 * u - LANES, 0)
            skip = lo - (1024 * u - LANES)
            both = product(
                rowcut[:, lo:end], col_band[skip : skip + end - lo, :], ((1,), (0,))
            )
            if u == 4:
                both = both + product(
                    rowcut[:, :LANES], col_band[10 * LANES :, :], ((1,), (0,))
                )
            cut[:, LANES * u : LANES * (u + 1)] = both[: COLS * SLOT] + both[COLS * SLOT :]
            if u == 3:
                pl.semaphore_wait(barrier, len(GROUP_A + GROUP_B + GROUP_C) + 2)
                for k in GROUP_A:
                    signal(group_ready, peer(k))
                for copy in early:
                    copy.start()
    for copy in late:
        copy.start()
    near = early + late
    pl.semaphore_wait(group_ready, len(GROUP_A))
    for k in GROUP_B:
        signal(all_ready, peer(k))
    gathered[q] = cut[pl.ds(pl.multiple_of(q * SLOT, 8), SLOT), :]
    for copy in loads[2:]:
        copy.wait()
    for step in range(1, COLS):
        source = (q + step) & 3
        for part, (lo, size) in enumerate(((0, 4 * LANES), (4 * LANES, LANES))):
            block = gathered.at[source, :, pl.ds(lo, size)]
            pltpu.make_async_copy(block, block, near_recv.at[source, part]).wait()

    row_id = lax.broadcasted_iota(jnp.int32, (8, LANES), 0)

    @pl.when((q == 0) | (q == 3))
    def _():
        for source in range(COLS):
            for row in range(2):
                line = border.at[source, pl.ds(row, 1), :]
                pltpu.make_async_copy(line, line, edge_recv.at[source, row]).wait()
        valid = ((q == 0) & (p > 0)) | ((q == 3) & (p < ROWS - 1))
        keep = jnp.where(valid, 2, 0)
        for t, tile in enumerate(joined([border[source] for source in range(COLS)])):
            edges[:, LANES * t : LANES * (t + 1)] = jnp.where(row_id < keep, tile, 0.0)

    for s in range(3):
        rows = slice(8 * s, 8 * s + 8)
        points = joined([gathered[source, rows, :] for source in range(COLS)])
        if s == 2:
            points = [jnp.where(row_id < 2, x, 0.0) for x in points]
        if s != 1:
            flag = jnp.where(q == (0 if s == 0 else 3), 1.0, 0.0).astype(jnp.float32)
            points = [
                x + flag * edges[:, LANES * t : LANES * (t + 1)] for t, x in enumerate(points)
            ]
        points = [
            x * row_window[rows, :] * common[2 + t // 3, 8 * (t % 3) : 8 * (t % 3) + 8, :]
            for t, x in enumerate(points)
        ]
        for freq, (real, imag) in enumerate(real_eighteen(points)):
            at = (freq // HALF) * 256 + (freq % HALF) * SLOT + 8 * s
            cos, sin = common[0, freq : freq + 1, :], common[1, freq : freq + 1, :]
            if imag is None:
                turned[at : at + 8, :LANES] = real * cos
                turned[at : at + 8, LANES:] = -real * sin
            else:
                turned[at : at + 8, :LANES] = real * cos + imag * sin
                turned[at : at + 8, LANES:] = imag * cos - real * sin

    first_high, first_low = matrices[:LANES, :], matrices[LANES : 2 * LANES, :]
    for h in range(2):
        high, low = halves(turned[256 * h : 256 * (h + 1), :])
        both = (
            product(first_high, low, ((1,), (1,)))
            + product(first_low, high, ((1,), (1,)))
            + product(first_high, high, ((1,), (1,)))
        )
        leaving[0, :, 256 * h : 256 * (h + 1)] = both[: LANES // 2]
        leaving[1, :, 256 * h : 256 * (h + 1)] = both[LANES // 2 :]

    def block_of(other):
        lanes = pl.multiple_of((other & 1) * 256, 256)
        return leaving.at[:, pl.ds(other >> 1, 1), pl.ds(lanes, 256)]

    pl.semaphore_wait(all_ready, len(GROUP_B))
    def far(k):
        other = me ^ k
        pltpu.make_async_remote_copy(
            src_ref=block_of(other),
            dst_ref=arrived.at[:, pl.ds(me, 1), :],
            send_sem=far_send,
            recv_sem=far_recv,
            device_id=(other >> 2, other & 3),
            device_id_type=MESH,
        ).start()

    for lo, hi in ((0, FARTHEST), (FARTHEST + 1, DEVICES)):

        @pl.loop(lo, hi)
        def _(step):
            far(step ^ FARTHEST)

    pltpu.make_async_copy(block_of(me), arrived.at[:, pl.ds(me, 1), :], far_recv).start()
    pltpu.make_async_copy(arrived, arrived, far_recv).wait()

    wave_high, wave_low = matrices[2 * LANES : 4 * LANES, :], matrices[4 * LANES :, :]
    high, low = halves(arrived[...].reshape(2 * DEVICES, 256).T)
    both = (
        product(low, wave_high, ((1,), (0,)))
        + product(high, wave_low, ((1,), (0,)))
        + product(high, wave_high, ((1,), (0,)))
    )
    mixed[0], mixed[1] = both[:, :LANES], both[:, LANES:]
    real_points, imag_points = [], []
    for r in range(RADIX):
        real = mixed[0, pl.ds(r, HALF, stride=SLOT), :]
        imag = mixed[1, pl.ds(r, HALF, stride=SLOT), :]
        cos, sin = common[0, r : r + 1, :], common[1, r : r + 1, :]
        real_points.append(real * cos + imag * sin)
        imag_points.append(imag * cos - real * sin)
    for freq, (real, imag) in enumerate(complex_eighteen(real_points, imag_points)):
        power[:, LANES * freq : LANES * (freq + 1)] = (real * real + imag * imag) * np.float32(
            8.0 / (LENGTH * LENGTH)
        )

    for copy in near:
        copy.wait_send()
    pltpu.make_async_copy(filler, filler, far_send).wait()


def local(field):
    constants = tables()
    anywhere = pl.BlockSpec(memory_space=pltpu.HBM)
    f32, bf16 = jnp.float32, jnp.bfloat16
    power = pl.pallas_call(
        kernel,
        out_shape=jax.ShapeDtypeStruct((HALF, LENGTH), f32),
        in_specs=[anywhere] * (1 + len(constants)),
        out_specs=pl.BlockSpec(memory_space=pltpu.VMEM),
        scratch_shapes=[
            pltpu.VMEM((RAW_ROWS, RAW_COLS), bf16),
            pltpu.VMEM((COLS * SLOT, WIDE), bf16),
            pltpu.VMEM(constants[1].shape, bf16),
            pltpu.VMEM(constants[2].shape, bf16),
            pltpu.VMEM((2 + RADIX // 3, SLOT, LANES), f32),
            pltpu.VMEM((SLOT, LANES), f32),
            pltpu.VMEM((2 * COLS * SLOT, RAW_COLS), bf16),
            pltpu.VMEM((COLS * SLOT, WIDE), f32),
            pltpu.VMEM((COLS, SLOT, WIDE), f32),
            pltpu.VMEM((COLS, 8, WIDE), f32),
            pltpu.VMEM((8, LENGTH), f32),
            pltpu.VMEM((512, 256), f32),
            pltpu.VMEM((2, LANES // 2, 512), f32),
            pltpu.VMEM((2, DEVICES, 256), f32),
            pltpu.VMEM((2, 256, LANES), f32),
            pltpu.VMEM((DEVICES - 1, 4, LANES), f32),
            pltpu.SemaphoreType.DMA((len(CHUNKS) + 5,)),
            pltpu.SemaphoreType.DMA((COLS, 2)),
            pltpu.SemaphoreType.DMA((COLS, 2)),
            pltpu.SemaphoreType.DMA((2, 2)),
            pltpu.SemaphoreType.DMA((COLS, 2)),
            pltpu.SemaphoreType.DMA,
            pltpu.SemaphoreType.DMA,
            pltpu.SemaphoreType.REGULAR,
            pltpu.SemaphoreType.REGULAR,
        ],
        compiler_params=pltpu.CompilerParams(
            collective_id=0, has_side_effects=True, vmem_limit_bytes=64 * 2**20 - 200 * 2**10
        ),
    )(field, *[jnp.asarray(c) for c in constants])
    return power[None]


def solution(mesh):
    return jax.shard_map(
        local,
        mesh=mesh,
        in_specs=(P(None, "rows", "cols"),),
        out_specs=P(None, ("rows", "cols"), None),
        check_vma=False,
    )
```

```python
import jax
import jax.numpy as jnp
import ml_dtypes
import numpy as np
from jax import lax
from jax.experimental import pallas as pl
from jax.experimental.pallas import tpu as pltpu
from jax.sharding import PartitionSpec as P

TAPS = 33
STRIDE = 8
REACH = TAPS // 2
MESH = pl.DeviceIdType.MESH

ROWS, COLS = 32, 4
DEVICES = ROWS * COLS
LENGTH = 2304
RADIX = LENGTH // DEVICES
RAW_ROWS = LENGTH * STRIDE // ROWS
RAW_COLS = LENGTH * STRIDE // COLS
OUT_COLS = RAW_COLS // STRIDE
SLOT = 24
LANES = 128
WIDE = 5 * LANES
HALF = RADIX // 2


FARTHEST = 74
GROUP_A = [1, 2, 3]
GROUP_B = [4 * k for k in range(1, 8)]
GROUP_C = [32, 64, 96]
CUTS = [0, 640] + [640 + 512 * t for t in range(1, 8)] + [RAW_COLS]
CHUNKS = list(zip(CUTS[:-1], CUTS[1:]))


def taps_table():
    tap_ids = np.arange(TAPS, dtype=np.float32)
    shaped = np.sinc((tap_ids - np.float32(REACH)) / np.float32(STRIDE)).astype(np.float32)
    shaped = shaped * (
        np.float32(0.54)
        - np.float32(0.46) * np.cos(np.float32(2 * np.pi) * tap_ids / np.float32(TAPS - 1))
    )
    shaped = shaped / np.sum(shaped)
    return shaped.astype(ml_dtypes.bfloat16).astype(np.float32)


def tap_at(offset):
    taps = taps_table()
    inside = (offset >= 0) & (offset < TAPS)
    return np.where(inside, taps[np.clip(offset, 0, TAPS - 1)], 0).astype(ml_dtypes.bfloat16)


def split(matrix):
    high = matrix.astype(ml_dtypes.bfloat16)
    low = (matrix - high.astype(np.float64)).astype(ml_dtypes.bfloat16)
    return high, low


def tables():
    own = np.full((COLS, SLOT), -(10**6))
    own[:, :RADIX] = RADIX * np.arange(COLS)[:, None] + np.arange(RADIX)
    own[0, RADIX : RADIX + 2] = [-2, -1]
    own[-1, RADIX : RADIX + 2] = [COLS * RADIX, COLS * RADIX + 1]
    raw = np.arange(RAW_ROWS)
    row_band = tap_at(raw[None, :] - STRIDE * own.reshape(-1, 1) + REACH)

    lane = np.arange(LANES)
    inner = tap_at(np.arange(10 * LANES)[:, None] - LANES - STRIDE * lane[None, :] + REACH)
    edge = tap_at(lane[:, None] - STRIDE * (lane[None, :] - LANES) + REACH)
    col_band = np.concatenate([inner, edge], axis=0)

    angle = 2 * np.pi / LANES * (lane[:, None] * lane[None, :] % LANES)
    cos, sin = np.cos(angle), np.sin(angle)
    wave = np.block([[cos, -sin], [sin, cos]])
    first = np.concatenate([wave[:, : LANES // 2], wave[:, LANES : LANES + LANES // 2]], axis=1).T
    matrices = np.concatenate(split(first) + split(wave), axis=0)

    turn = 2 * np.pi / LENGTH * (np.arange(RADIX)[:, None] * lane[None, :])
    twiddles = np.stack([np.cos(turn), np.sin(turn)]).astype(np.float32)

    window = 0.5 - 0.5 * np.cos(2 * np.pi * np.arange(LENGTH) / LENGTH)
    row_window = np.zeros((DEVICES, SLOT))
    row_window[:, :RADIX] = window.reshape(DEVICES, RADIX)
    row_window = np.broadcast_to(row_window[:, :, None], (DEVICES, SLOT, LANES))
    col_window = np.broadcast_to(window.reshape(RADIX, 1, LANES), (RADIX, 8, LANES))
    twiddles = np.pad(twiddles, ((0, 0), (0, SLOT - RADIX), (0, 0)))
    floats = np.concatenate([row_window, twiddles, col_window.reshape(-1, SLOT, LANES)], axis=0)
    row_band = np.pad(row_band, ((0, COLS * SLOT), (0, WIDE - RAW_ROWS)))
    return row_band, col_band, matrices, floats.astype(np.float32)


def real_nine(points):
    sums = [points[m] + points[9 - m] for m in range(1, 5)]
    gaps = [points[m] - points[9 - m] for m in range(1, 5)]
    reals, imags = [points[0] + sums[0] + sums[1] + sums[2] + sums[3]], [None]
    for freq in range(1, 5):
        real, imag = points[0], None
        for m in range(1, 5):
            phase = 2 * np.pi * (m * freq % 9) / 9
            real = real + sums[m - 1] * np.float32(np.cos(phase))
            term = gaps[m - 1] * np.float32(-np.sin(phase))
            imag = term if imag is None else imag + term
        reals.append(real)
        imags.append(imag)
    return reals, imags


def folded(points):
    evens = [points[2 * b % 18] for b in range(9)]
    odds = [points[(9 + 2 * b) % 18] for b in range(9)]
    return (
        real_nine([x + y for x, y in zip(evens, odds)]),
        real_nine([x - y for x, y in zip(evens, odds)]),
    )


def real_eighteen(points):
    both = folded(points)
    out = []
    for freq in range(18):
        reals, imags = both[freq % 2]
        at = freq % 9
        if at == 0:
            out.append((reals[0], None))
        elif at <= 4:
            out.append((reals[at], imags[at]))
        else:
            out.append((reals[9 - at], -imags[9 - at]))
    return out


def complex_eighteen(real_points, imag_points):
    both_real, both_imag = folded(real_points), folded(imag_points)
    out = []
    for freq in range(18):
        (a_re, a_im), (b_re, b_im) = both_real[freq % 2], both_imag[freq % 2]
        at = freq % 9
        if at == 0:
            out.append((a_re[0], b_re[0]))
        elif at <= 4:
            out.append((a_re[at] - b_im[at], a_im[at] + b_re[at]))
        else:
            out.append((a_re[9 - at] + b_im[9 - at], b_re[9 - at] - a_im[9 - at]))
    return out


def halves(value):
    high = value.astype(jnp.bfloat16)
    low = (value - high.astype(jnp.float32)).astype(jnp.bfloat16)
    return high, low


def product(left, right, dims):
    return lax.dot_general(left, right, (dims, ((), ())), preferred_element_type=jnp.float32)


def joined(blocks):
    lane = lax.broadcasted_iota(jnp.int32, (8, LANES), 1)
    turned = [pltpu.roll(b, 64, 1) if i % 2 else b for i, b in enumerate(blocks)]
    part = [[b[:, LANES * t : LANES * (t + 1)] for t in range(5)] for b in turned]
    zero = jnp.zeros((8, LANES), jnp.float32)
    out = part[0][:4]
    out.append(jnp.where(lane < 66, part[0][4], zero) + jnp.where(lane >= 62, part[1][0], zero))
    out += part[1][1:4]
    out.append(part[1][4] + jnp.where(lane >= 126, part[2][4], zero))
    out.append(part[2][0] + jnp.where(lane < 2, part[1][0], zero))
    out += part[2][1:4]
    out.append(jnp.where(lane < 66, part[2][4], zero) + jnp.where(lane >= 62, part[3][0], zero))
    out += part[3][1:5]
    return out


def kernel(
    field, row_band_in, col_band_in, matrices_in, floats_in,
    power,
    raw, row_band, col_band, matrices, common, row_window,
    rowcut, cut, gathered, border, edges, turned, leaving, arrived, mixed, filler,
    load_sem, near_send, near_recv, edge_send, edge_recv, far_send, far_recv, group_ready, all_ready,
):
    p, q = lax.axis_index("rows"), lax.axis_index("cols")
    me = p * COLS + q
    def peer(k):
        return (p ^ (k >> 2), q ^ (k & 3))

    small = len(CHUNKS)
    loads = [
        pltpu.make_async_copy(row_band_in.at[pl.ds(0, COLS * SLOT)], row_band, load_sem.at[small]),
        pltpu.make_async_copy(col_band_in, col_band, load_sem.at[small + 1]),
        pltpu.make_async_copy(matrices_in, matrices, load_sem.at[small + 2]),
        pltpu.make_async_copy(floats_in.at[me], row_window, load_sem.at[small + 3]),
        pltpu.make_async_copy(
            floats_in.at[pl.ds(DEVICES, 2 + RADIX // 3)], common, load_sem.at[small + 4]
        ),
    ]
    field_loads = [
        pltpu.make_async_copy(
            field.at[0, :, pl.ds(lo, hi - lo)], raw.at[:, pl.ds(lo, hi - lo)], load_sem.at[t]
        )
        for t, (lo, hi) in enumerate(CHUNKS)
    ]
    for copy in loads[:1] + field_loads[:2] + loads[1:2]:
        copy.start()

    def signal(semaphore, device):
        pl.semaphore_signal(semaphore, inc=1, device_id=device, device_id_type=MESH)

    barrier = pltpu.get_barrier_semaphore()
    for k in GROUP_C + GROUP_B + GROUP_A:
        signal(barrier, peer(k))
    for side, to_p in ((0, (p + 31) & 31), (3, (p + 1) & 31)):

        @pl.when(q == side)
        def _():
            for to_q in range(COLS):
                signal(barrier, (to_p, to_q))

    for copy in field_loads[2:] + loads[2:]:
        copy.start()

    for row in (HALF * SLOT, 256 + HALF * SLOT):
        turned[pl.ds(row, 256 - HALF * SLOT), :] = jnp.zeros((256 - HALF * SLOT, 256), jnp.float32)
    edges[...] = jnp.zeros_like(edges)

    def row_copy(step, part, lo, size):
        to = (q + step) & 3
        return pltpu.make_async_remote_copy(
            src_ref=cut.at[pl.ds(pl.multiple_of(to * SLOT, 8), SLOT), pl.ds(lo, size)],
            dst_ref=gathered.at[q, :, pl.ds(lo, size)],
            send_sem=near_send.at[step, part],
            recv_sem=near_recv.at[q, part],
            device_id=(p, to),
            device_id_type=MESH,
        )

    def edge_copy(side, row):
        return pltpu.make_async_remote_copy(
            src_ref=cut.at[pl.ds((3 * SLOT, 0)[side] + RADIX + row, 1), :],
            dst_ref=border.at[q, pl.ds(row, 1), :],
            send_sem=edge_send.at[side, row],
            recv_sem=edge_recv.at[q, row],
            device_id=(((p + 1) & 31, 3 * 0), ((p + 31) & 31, 3))[side],
            device_id_type=MESH,
        )

    early = [row_copy(step, 0, 0, 4 * LANES) for step in (2, 1, 3)]
    late = [row_copy(step, 1, 4 * LANES, LANES) for step in (2, 1, 3)]
    late += [edge_copy(side, row) for side in range(2) for row in range(2)]

    loads[0].wait()
    for t, (begin, end) in enumerate(CHUNKS):
        field_loads[t].wait()
        part = product(row_band[:, :RAW_ROWS], raw[:, begin:end], ((1,), (0,)))
        high, low = halves(part)
        rowcut[: COLS * SLOT, begin:end] = high
        rowcut[COLS * SLOT :, begin:end] = low
        for u in range(5):
            if min(1024 * u + 1024 + LANES, RAW_COLS) != end:
                continue
            if u == 0:
                loads[1].wait()
            lo = max(1024 * u - LANES, 0)
            skip = lo - (1024 * u - LANES)
            both = product(
                rowcut[:, lo:end], col_band[skip : skip + end - lo, :], ((1,), (0,))
            )
            if u == 4:
                both = both + product(
                    rowcut[:, :LANES], col_band[10 * LANES :, :], ((1,), (0,))
                )
            cut[:, LANES * u : LANES * (u + 1)] = both[: COLS * SLOT] + both[COLS * SLOT :]
            if u == 3:
                pl.semaphore_wait(barrier, len(GROUP_A + GROUP_B + GROUP_C) + 2)
                for k in GROUP_A:
                    signal(group_ready, peer(k))
                for copy in early:
                    copy.start()
    for copy in late:
        copy.start()
    near = early + late
    pl.semaphore_wait(group_ready, len(GROUP_A))
    for k in GROUP_B:
        signal(all_ready, peer(k))
    gathered[q] = cut[pl.ds(pl.multiple_of(q * SLOT, 8), SLOT), :]
    for copy in loads[2:]:
        copy.wait()
    for step in range(1, COLS):
        source = (q + step) & 3
        for part, (lo, size) in enumerate(((0, 4 * LANES), (4 * LANES, LANES))):
            block = gathered.at[source, :, pl.ds(lo, size)]
            pltpu.make_async_copy(block, block, near_recv.at[source, part]).wait()

    row_id = lax.broadcasted_iota(jnp.int32, (8, LANES), 0)

    @pl.when((q == 0) | (q == 3))
    def _():
        for source in range(COLS):
            for row in range(2):
                line = border.at[source, pl.ds(row, 1), :]
                pltpu.make_async_copy(line, line, edge_recv.at[source, row]).wait()
        valid = ((q == 0) & (p > 0)) | ((q == 3) & (p < ROWS - 1))
        keep = jnp.where(valid, 2, 0)
        for t, tile in enumerate(joined([border[source] for source in range(COLS)])):
            edges[:, LANES * t : LANES * (t + 1)] = jnp.where(row_id < keep, tile, 0.0)

    for s in range(3):
        rows = slice(8 * s, 8 * s + 8)
        points = joined([gathered[source, rows, :] for source in range(COLS)])
        if s == 2:
            points = [jnp.where(row_id < 2, x, 0.0) for x in points]
        if s != 1:
            flag = jnp.where(q == (0 if s == 0 else 3), 1.0, 0.0).astype(jnp.float32)
            points = [
                x + flag * edges[:, LANES * t : LANES * (t + 1)] for t, x in enumerate(points)
            ]
        points = [
            x * row_window[rows, :] * common[2 + t // 3, 8 * (t % 3) : 8 * (t % 3) + 8, :]
            for t, x in enumerate(points)
        ]
        for freq, (real, imag) in enumerate(real_eighteen(points)):
            at = (freq // HALF) * 256 + (freq % HALF) * SLOT + 8 * s
            cos, sin = common[0, freq : freq + 1, :], common[1, freq : freq + 1, :]
            if imag is None:
                turned[at : at + 8, :LANES] = real * cos
                turned[at : at + 8, LANES:] = -real * sin
            else:
                turned[at : at + 8, :LANES] = real * cos + imag * sin
                turned[at : at + 8, LANES:] = imag * cos - real * sin

    first_high, first_low = matrices[:LANES, :], matrices[LANES : 2 * LANES, :]
    for h in range(2):
        high, low = halves(turned[256 * h : 256 * (h + 1), :])
        both = (
            product(first_high, low, ((1,), (1,)))
            + product(first_low, high, ((1,), (1,)))
            + product(first_high, high, ((1,), (1,)))
        )
        leaving[0, :, 256 * h : 256 * (h + 1)] = both[: LANES // 2]
        leaving[1, :, 256 * h : 256 * (h + 1)] = both[LANES // 2 :]

    def block_of(other):
        lanes = pl.multiple_of((other & 1) * 256, 256)
        return leaving.at[:, pl.ds(other >> 1, 1), pl.ds(lanes, 256)]

    pl.semaphore_wait(all_ready, len(GROUP_B))
    def far(k):
        other = me ^ k
        pltpu.make_async_remote_copy(
            src_ref=block_of(other),
            dst_ref=arrived.at[:, pl.ds(me, 1), :],
            send_sem=far_send,
            recv_sem=far_recv,
            device_id=(other >> 2, other & 3),
            device_id_type=MESH,
        ).start()

    for lo, hi in ((0, FARTHEST), (FARTHEST + 1, DEVICES)):

        @pl.loop(lo, hi)
        def _(step):
            far(step ^ FARTHEST)

    pltpu.make_async_copy(block_of(me), arrived.at[:, pl.ds(me, 1), :], far_recv).start()
    pltpu.make_async_copy(arrived, arrived, far_recv).wait()

    wave_high, wave_low = matrices[2 * LANES : 4 * LANES, :], matrices[4 * LANES :, :]
    high, low = halves(arrived[...].reshape(2 * DEVICES, 256).T)
    both = (
        product(low, wave_high, ((1,), (0,)))
        + product(high, wave_low, ((1,), (0,)))
        + product(high, wave_high, ((1,), (0,)))
    )
    mixed[0], mixed[1] = both[:, :LANES], both[:, LANES:]
    real_points, imag_points = [], []
    for r in range(RADIX):
        real = mixed[0, pl.ds(r, HALF, stride=SLOT), :]
        imag = mixed[1, pl.ds(r, HALF, stride=SLOT), :]
        cos, sin = common[0, r : r + 1, :], common[1, r : r + 1, :]
        real_points.append(real * cos + imag * sin)
        imag_points.append(imag * cos - real * sin)
    for freq, (real, imag) in enumerate(complex_eighteen(real_points, imag_points)):
        power[:, LANES * freq : LANES * (freq + 1)] = (real * real + imag * imag) * np.float32(
            8.0 / (LENGTH * LENGTH)
        )

    for copy in near:
        copy.wait_send()
    pltpu.make_async_copy(filler, filler, far_send).wait()


def local(field):
    constants = tables()
    anywhere = pl.BlockSpec(memory_space=pltpu.HBM)
    f32, bf16 = jnp.float32, jnp.bfloat16
    power = pl.pallas_call(
        kernel,
        out_shape=jax.ShapeDtypeStruct((HALF, LENGTH), f32),
        in_specs=[anywhere] * (1 + len(constants)),
        out_specs=pl.BlockSpec(memory_space=pltpu.VMEM),
        scratch_shapes=[
            pltpu.VMEM((RAW_ROWS, RAW_COLS), bf16),
            pltpu.VMEM((COLS * SLOT, WIDE), bf16),
            pltpu.VMEM(constants[1].shape, bf16),
            pltpu.VMEM(constants[2].shape, bf16),
            pltpu.VMEM((2 + RADIX // 3, SLOT, LANES), f32),
            pltpu.VMEM((SLOT, LANES), f32),
            pltpu.VMEM((2 * COLS * SLOT, RAW_COLS), bf16),
            pltpu.VMEM((COLS * SLOT, WIDE), f32),
            pltpu.VMEM((COLS, SLOT, WIDE), f32),
            pltpu.VMEM((COLS, 8, WIDE), f32),
            pltpu.VMEM((8, LENGTH), f32),
            pltpu.VMEM((512, 256), f32),
            pltpu.VMEM((2, LANES // 2, 512), f32),
            pltpu.VMEM((2, DEVICES, 256), f32),
            pltpu.VMEM((2, 256, LANES), f32),
            pltpu.VMEM((DEVICES - 1, 4, LANES), f32),
            pltpu.SemaphoreType.DMA((len(CHUNKS) + 5,)),
            pltpu.SemaphoreType.DMA((COLS, 2)),
            pltpu.SemaphoreType.DMA((COLS, 2)),
            pltpu.SemaphoreType.DMA((2, 2)),
            pltpu.SemaphoreType.DMA((COLS, 2)),
            pltpu.SemaphoreType.DMA,
            pltpu.SemaphoreType.DMA,
            pltpu.SemaphoreType.REGULAR,
            pltpu.SemaphoreType.REGULAR,
        ],
        compiler_params=pltpu.CompilerParams(
            collective_id=0, has_side_effects=True, vmem_limit_bytes=54936 * 2**10
        ),
    )(field, *[jnp.asarray(c) for c in constants])
    return power[None]


def solution(mesh):
    return jax.shard_map(
        local,
        mesh=mesh,
        in_specs=(P(None, "rows", "cols"),),
        out_specs=P(None, ("rows", "cols"), None),
        check_vma=False,
    )
```

```python
import jax
import jax.numpy as jnp
import ml_dtypes
import numpy as np
from jax import lax
from jax.experimental import pallas as pl
from jax.experimental.pallas import tpu as pltpu
from jax.sharding import PartitionSpec as P

TAPS = 33
STRIDE = 8
REACH = TAPS // 2
MESH = pl.DeviceIdType.MESH

ROWS, COLS = 32, 4
DEVICES = ROWS * COLS
LENGTH = 2304
RADIX = LENGTH // DEVICES
RAW_ROWS = LENGTH * STRIDE // ROWS
RAW_COLS = LENGTH * STRIDE // COLS
OUT_COLS = RAW_COLS // STRIDE
SLOT = 24
LANES = 128
WIDE = 5 * LANES
HALF = RADIX // 2


FARTHEST = 74
NEARNESS = 2


def bend(place):
    return (place & 1) + 2 * ((place >> 1) & (1 - (place & 1)))


def hops(device):
    y = (device & 2) + ((device >> 4) & 1)
    return bend((device >> 2) & 3) + bend((device >> 5) & 3) + bend(y)


NEAR_ORIGIN = sorted((d for d in range(DEVICES) if hops(d) <= NEARNESS), key=hops)
GROUP_A = [1, 2, 3]
GROUP_B = [4 * k for k in range(1, 8)]
GROUP_C = [32, 64, 96]
CUTS = [0] + [LANES + 1024 * t for t in range(5)] + [RAW_COLS]
CHUNKS = list(zip(CUTS[:-1], CUTS[1:]))


def taps_table():
    tap_ids = np.arange(TAPS, dtype=np.float32)
    shaped = np.sinc((tap_ids - np.float32(REACH)) / np.float32(STRIDE)).astype(np.float32)
    shaped = shaped * (
        np.float32(0.54)
        - np.float32(0.46) * np.cos(np.float32(2 * np.pi) * tap_ids / np.float32(TAPS - 1))
    )
    shaped = shaped / np.sum(shaped)
    return shaped.astype(ml_dtypes.bfloat16).astype(np.float32)


def tap_at(offset):
    taps = taps_table()
    inside = (offset >= 0) & (offset < TAPS)
    return np.where(inside, taps[np.clip(offset, 0, TAPS - 1)], 0).astype(ml_dtypes.bfloat16)


def split(matrix):
    high = matrix.astype(ml_dtypes.bfloat16)
    low = (matrix - high.astype(np.float64)).astype(ml_dtypes.bfloat16)
    return high, low


def tables():
    own = np.full((COLS, SLOT), -(10**6))
    own[:, :RADIX] = RADIX * np.arange(COLS)[:, None] + np.arange(RADIX)
    own[0, RADIX : RADIX + 2] = [-2, -1]
    own[-1, RADIX : RADIX + 2] = [COLS * RADIX, COLS * RADIX + 1]
    raw = np.arange(RAW_ROWS)
    row_band = tap_at(raw[None, :] - STRIDE * own.reshape(-1, 1) + REACH)

    lane = np.arange(LANES)
    inner = tap_at(np.arange(10 * LANES)[:, None] - LANES - STRIDE * lane[None, :] + REACH)
    edge = tap_at(lane[:, None] - STRIDE * (lane[None, :] - LANES) + REACH)
    col_band = np.concatenate([inner, edge], axis=0)

    angle = 2 * np.pi / LANES * (lane[:, None] * lane[None, :] % LANES)
    cos, sin = np.cos(angle), np.sin(angle)
    wave = np.block([[cos, -sin], [sin, cos]])
    first = np.concatenate([wave[:, : LANES // 2], wave[:, LANES : LANES + LANES // 2]], axis=1).T
    matrices = np.concatenate(split(first) + split(wave), axis=0)

    turn = 2 * np.pi / LENGTH * (np.arange(RADIX)[:, None] * lane[None, :])
    twiddles = np.stack([np.cos(turn), np.sin(turn)]).astype(np.float32)

    window = 0.5 - 0.5 * np.cos(2 * np.pi * np.arange(LENGTH) / LENGTH)
    row_window = np.zeros((DEVICES, SLOT))
    row_window[:, :RADIX] = window.reshape(DEVICES, RADIX)
    row_window = np.broadcast_to(row_window[:, :, None], (DEVICES, SLOT, LANES))
    col_window = np.broadcast_to(window.reshape(RADIX, 1, LANES), (RADIX, 8, LANES))
    twiddles = np.pad(twiddles, ((0, 0), (0, SLOT - RADIX), (0, 0)))
    floats = np.concatenate([row_window, twiddles, col_window.reshape(-1, SLOT, LANES)], axis=0)
    row_band = np.pad(row_band, ((0, COLS * SLOT), (0, WIDE - RAW_ROWS)))
    return row_band, col_band, matrices, floats.astype(np.float32)


def real_nine(points):
    sums = [points[m] + points[9 - m] for m in range(1, 5)]
    gaps = [points[m] - points[9 - m] for m in range(1, 5)]
    reals, imags = [points[0] + sums[0] + sums[1] + sums[2] + sums[3]], [None]
    for freq in range(1, 5):
        real, imag = points[0], None
        for m in range(1, 5):
            phase = 2 * np.pi * (m * freq % 9) / 9
            real = real + sums[m - 1] * np.float32(np.cos(phase))
            term = gaps[m - 1] * np.float32(-np.sin(phase))
            imag = term if imag is None else imag + term
        reals.append(real)
        imags.append(imag)
    return reals, imags


def folded(points):
    evens = [points[2 * b % 18] for b in range(9)]
    odds = [points[(9 + 2 * b) % 18] for b in range(9)]
    return (
        real_nine([x + y for x, y in zip(evens, odds)]),
        real_nine([x - y for x, y in zip(evens, odds)]),
    )


def real_eighteen(points):
    both = folded(points)
    out = []
    for freq in range(18):
        reals, imags = both[freq % 2]
        at = freq % 9
        if at == 0:
            out.append((reals[0], None))
        elif at <= 4:
            out.append((reals[at], imags[at]))
        else:
            out.append((reals[9 - at], -imags[9 - at]))
    return out


def complex_eighteen(real_points, imag_points):
    both_real, both_imag = folded(real_points), folded(imag_points)
    out = []
    for freq in range(18):
        (a_re, a_im), (b_re, b_im) = both_real[freq % 2], both_imag[freq % 2]
        at = freq % 9
        if at == 0:
            out.append((a_re[0], b_re[0]))
        elif at <= 4:
            out.append((a_re[at] - b_im[at], a_im[at] + b_re[at]))
        else:
            out.append((a_re[9 - at] + b_im[9 - at], b_re[9 - at] - a_im[9 - at]))
    return out


def halves(value):
    high = value.astype(jnp.bfloat16)
    low = (value - high.astype(jnp.float32)).astype(jnp.bfloat16)
    return high, low


def product(left, right, dims):
    return lax.dot_general(left, right, (dims, ((), ())), preferred_element_type=jnp.float32)


def joined(blocks):
    lane = lax.broadcasted_iota(jnp.int32, (8, LANES), 1)
    turned = [pltpu.roll(b, 64, 1) if i % 2 else b for i, b in enumerate(blocks)]
    part = [[b[:, LANES * t : LANES * (t + 1)] for t in range(5)] for b in turned]
    zero = jnp.zeros((8, LANES), jnp.float32)
    out = part[0][:4]
    out.append(jnp.where(lane < 66, part[0][4], zero) + jnp.where(lane >= 62, part[1][0], zero))
    out += part[1][1:4]
    out.append(part[1][4] + jnp.where(lane >= 126, part[2][4], zero))
    out.append(part[2][0] + jnp.where(lane < 2, part[1][0], zero))
    out += part[2][1:4]
    out.append(jnp.where(lane < 66, part[2][4], zero) + jnp.where(lane >= 62, part[3][0], zero))
    out += part[3][1:5]
    return out


def kernel(
    field, row_band_in, col_band_in, matrices_in, floats_in,
    power,
    raw, row_band, col_band, matrices, common, row_window,
    rowcut, cut, gathered, border, edges, turned, leaving, arrived, mixed, filler,
    load_sem, near_send, near_recv, edge_send, edge_recv, far_send, far_recv, group_ready, all_ready,
):
    p, q = lax.axis_index("rows"), lax.axis_index("cols")
    me = p * COLS + q
    def peer(k):
        return (p ^ (k >> 2), q ^ (k & 3))

    small = len(CHUNKS)
    loads = [
        pltpu.make_async_copy(row_band_in.at[pl.ds(0, COLS * SLOT)], row_band, load_sem.at[small]),
        pltpu.make_async_copy(col_band_in, col_band, load_sem.at[small + 1]),
        pltpu.make_async_copy(matrices_in, matrices, load_sem.at[small + 2]),
        pltpu.make_async_copy(floats_in.at[me], row_window, load_sem.at[small + 3]),
        pltpu.make_async_copy(
            floats_in.at[pl.ds(DEVICES, 2 + RADIX // 3)], common, load_sem.at[small + 4]
        ),
    ]
    field_loads = [
        pltpu.make_async_copy(
            field.at[0, :, pl.ds(lo, hi - lo)], raw.at[:, pl.ds(lo, hi - lo)], load_sem.at[t]
        )
        for t, (lo, hi) in enumerate(CHUNKS)
    ]
    for copy in loads[:1] + field_loads[:2] + loads[1:2]:
        copy.start()

    def signal(semaphore, device):
        pl.semaphore_signal(semaphore, inc=1, device_id=device, device_id_type=MESH)

    barrier = pltpu.get_barrier_semaphore()
    for k in GROUP_C + GROUP_B + GROUP_A:
        signal(barrier, peer(k))
    has_above, has_below = p > 0, p < ROWS - 1

    @pl.when((q == 0) & has_above)
    def _():
        for to_q in range(COLS):
            signal(barrier, (p - 1, to_q))

    @pl.when((q == COLS - 1) & has_below)
    def _():
        for to_q in range(COLS):
            signal(barrier, (p + 1, to_q))

    for copy in field_loads[2:] + loads[2:]:
        copy.start()

    for row in (HALF * SLOT, 256 + HALF * SLOT):
        turned[pl.ds(row, 256 - HALF * SLOT), :] = jnp.zeros((256 - HALF * SLOT, 256), jnp.float32)
    edges[...] = jnp.zeros_like(edges)

    def row_copy(step, part, lo, size):
        to = (q + step) & 3
        return pltpu.make_async_remote_copy(
            src_ref=cut.at[pl.ds(pl.multiple_of(to * SLOT, 8), SLOT), pl.ds(lo, size)],
            dst_ref=gathered.at[q, :, pl.ds(lo, size)],
            send_sem=near_send.at[step, part],
            recv_sem=near_recv.at[q, part],
            device_id=(p, to),
            device_id_type=MESH,
        )

    def edge_copy(side, row):
        return pltpu.make_async_remote_copy(
            src_ref=cut.at[pl.ds((3 * SLOT, 0)[side] + RADIX + row, 1), :],
            dst_ref=border.at[q, pl.ds(row, 1), :],
            send_sem=edge_send.at[side, row],
            recv_sem=edge_recv.at[q, row],
            device_id=((p + 1, 0), (p - 1, COLS - 1))[side],
            device_id_type=MESH,
        )

    early = [row_copy(step, 0, 0, 4 * LANES) for step in (2, 1, 3)]
    late = [row_copy(step, 1, 4 * LANES, LANES) for step in (2, 1, 3)]
    edge = [[edge_copy(side, row) for row in range(2)] for side in range(2)]

    def filter_rows(begin, size):
        part = product(row_band[:, :RAW_ROWS], raw[:, pl.ds(begin, size)], ((1,), (0,)))
        high, low = halves(part)
        rowcut[: COLS * SLOT, pl.ds(begin + LANES, size)] = high
        rowcut[COLS * SLOT :, pl.ds(begin + LANES, size)] = low

    rowcut[:, :LANES] = jnp.zeros((2 * COLS * SLOT, LANES), jnp.bfloat16)
    loads[0].wait()
    field_loads[0].wait()
    filter_rows(0, LANES)
    loads[1].wait()

    @pl.loop(0, 4)
    def _(u):
        begin = pl.multiple_of(1024 * u, LANES)
        chunk = raw.at[:, pl.ds(begin + LANES, 1024)]
        pltpu.make_async_copy(chunk, chunk, load_sem.at[u + 1]).wait()
        filter_rows(begin + LANES, 1024)
        both = product(
            rowcut[:, pl.ds(begin, 10 * LANES)], col_band[: 10 * LANES, :], ((1,), (0,))
        )
        cut[:, pl.ds(pl.multiple_of(LANES * u, LANES), LANES)] = (
            both[: COLS * SLOT] + both[COLS * SLOT :]
        )

    pl.semaphore_wait(
        barrier,
        len(GROUP_A + GROUP_B + GROUP_C)
        + has_above.astype(jnp.int32)
        + has_below.astype(jnp.int32),
    )
    for k in GROUP_A:
        signal(group_ready, peer(k))
    for copy in early:
        copy.start()
    field_loads[5].wait()
    filter_rows(CUTS[5], RAW_COLS - CUTS[5])
    both = product(
        rowcut[:, 4096 : RAW_COLS + LANES], col_band[: RAW_COLS + LANES - 4096, :], ((1,), (0,))
    ) + product(rowcut[:, LANES : 2 * LANES], col_band[10 * LANES :, :], ((1,), (0,)))
    cut[:, 4 * LANES :] = both[: COLS * SLOT] + both[COLS * SLOT :]
    for copy in late:
        copy.start()
    for side, exists in enumerate((has_below, has_above)):

        @pl.when(exists)
        def _():
            for copy in edge[side]:
                copy.start()

    near = early + late
    pl.semaphore_wait(group_ready, len(GROUP_A))
    for k in GROUP_B:
        signal(all_ready, peer(k))
    gathered[q] = cut[pl.ds(pl.multiple_of(q * SLOT, 8), SLOT), :]
    for copy in loads[2:]:
        copy.wait()
    for step in range(1, COLS):
        source = (q + step) & 3
        for part, (lo, size) in enumerate(((0, 4 * LANES), (4 * LANES, LANES))):
            block = gathered.at[source, :, pl.ds(lo, size)]
            pltpu.make_async_copy(block, block, near_recv.at[source, part]).wait()

    row_id = lax.broadcasted_iota(jnp.int32, (8, LANES), 0)

    @pl.when(((q == 0) & has_above) | ((q == COLS - 1) & has_below))
    def _():
        for source in range(COLS):
            for row in range(2):
                line = border.at[source, pl.ds(row, 1), :]
                pltpu.make_async_copy(line, line, edge_recv.at[source, row]).wait()
        for t, tile in enumerate(joined([border[source] for source in range(COLS)])):
            edges[:, LANES * t : LANES * (t + 1)] = jnp.where(row_id < 2, tile, 0.0)

    @pl.loop(0, 3)
    def _(s):
        rows = pl.ds(pl.multiple_of(8 * s, 8), 8)
        points = joined([gathered[source, rows, :] for source in range(COLS)])
        limit = jnp.where(s == 2, RADIX - 16, 8)
        at_end = ((q == 0) & (s == 0)) | ((q == COLS - 1) & (s == 2))
        flag = jnp.where(at_end, 1.0, 0.0).astype(jnp.float32)
        mine = row_window[rows, :]
        for t in range(RADIX):
            point = jnp.where(row_id < limit, points[t], 0.0)
            point = point + flag * edges[:, LANES * t : LANES * (t + 1)]
            points[t] = point * mine * common[2 + t // 3, 8 * (t % 3) : 8 * (t % 3) + 8, :]
        for freq, (real, imag) in enumerate(real_eighteen(points)):
            at = (freq // HALF) * 256 + (freq % HALF) * SLOT
            out = pl.ds(pl.multiple_of(at + 8 * s, 8), 8)
            cos, sin = common[0, freq : freq + 1, :], common[1, freq : freq + 1, :]
            if imag is None:
                turned[out, :LANES] = real * cos
                turned[out, LANES:] = -real * sin
            else:
                turned[out, :LANES] = real * cos + imag * sin
                turned[out, LANES:] = imag * cos - real * sin

    first_high, first_low = matrices[:LANES, :], matrices[LANES : 2 * LANES, :]

    @pl.loop(0, 2)
    def _(h):
        part = pl.ds(pl.multiple_of(256 * h, 256), 256)
        high, low = halves(turned[part, :])
        both = (
            product(first_high, low, ((1,), (1,)))
            + product(first_low, high, ((1,), (1,)))
            + product(first_high, high, ((1,), (1,)))
        )
        leaving[0, :, part] = both[: LANES // 2]
        leaving[1, :, part] = both[LANES // 2 :]

    def block_of(other):
        lanes = pl.multiple_of((other & 1) * 256, 256)
        return leaving.at[:, pl.ds(other >> 1, 1), pl.ds(lanes, 256)]

    pl.semaphore_wait(all_ready, len(GROUP_B))
    def far(other):
        pltpu.make_async_remote_copy(
            src_ref=block_of(other),
            dst_ref=arrived.at[:, pl.ds(me, 1), :],
            send_sem=far_send,
            recv_sem=far_recv,
            device_id=(other >> 2, other & 3),
            device_id_type=MESH,
        ).start()

    for first in NEAR_ORIGIN:

        @pl.when(me != first)
        def _():
            far(jnp.int32(first))

    @pl.loop(0, DEVICES)
    def _(step):
        other = me ^ step ^ FARTHEST

        @pl.when((hops(other) > NEARNESS) & (other != me))
        def _():
            far(other)

    pltpu.make_async_copy(block_of(me), arrived.at[:, pl.ds(me, 1), :], far_recv).start()
    pltpu.make_async_copy(arrived, arrived, far_recv).wait()

    wave_high, wave_low = matrices[2 * LANES : 4 * LANES, :], matrices[4 * LANES :, :]
    high, low = halves(arrived[...].reshape(2 * DEVICES, 256).T)
    both = (
        product(low, wave_high, ((1,), (0,)))
        + product(high, wave_low, ((1,), (0,)))
        + product(high, wave_high, ((1,), (0,)))
    )
    mixed[0], mixed[1] = both[:, :LANES], both[:, LANES:]
    real_points, imag_points = [], []
    for r in range(RADIX):
        real = mixed[0, pl.ds(r, HALF, stride=SLOT), :]
        imag = mixed[1, pl.ds(r, HALF, stride=SLOT), :]
        cos, sin = common[0, r : r + 1, :], common[1, r : r + 1, :]
        real_points.append(real * cos + imag * sin)
        imag_points.append(imag * cos - real * sin)
    for freq, (real, imag) in enumerate(complex_eighteen(real_points, imag_points)):
        power[:, LANES * freq : LANES * (freq + 1)] = (real * real + imag * imag) * np.float32(
            8.0 / (LENGTH * LENGTH)
        )

    for copy in near:
        copy.wait_send()
    for side, exists in enumerate((has_below, has_above)):

        @pl.when(exists)
        def _():
            for copy in edge[side]:
                copy.wait_send()

    pltpu.make_async_copy(filler, filler, far_send).wait()


def local(field):
    constants = tables()
    anywhere = pl.BlockSpec(memory_space=pltpu.HBM)
    f32, bf16 = jnp.float32, jnp.bfloat16
    power = pl.pallas_call(
        kernel,
        out_shape=jax.ShapeDtypeStruct((HALF, LENGTH), f32),
        in_specs=[anywhere] * (1 + len(constants)),
        out_specs=pl.BlockSpec(memory_space=pltpu.VMEM),
        scratch_shapes=[
            pltpu.VMEM((RAW_ROWS, RAW_COLS), bf16),
            pltpu.VMEM((COLS * SLOT, WIDE), bf16),
            pltpu.VMEM(constants[1].shape, bf16),
            pltpu.VMEM(constants[2].shape, bf16),
            pltpu.VMEM((2 + RADIX // 3, SLOT, LANES), f32),
            pltpu.VMEM((SLOT, LANES), f32),
            pltpu.VMEM((2 * COLS * SLOT, RAW_COLS + LANES), bf16),
            pltpu.VMEM((COLS * SLOT, WIDE), f32),
            pltpu.VMEM((COLS, SLOT, WIDE), f32),
            pltpu.VMEM((COLS, 8, WIDE), f32),
            pltpu.VMEM((8, LENGTH), f32),
            pltpu.VMEM((512, 256), f32),
            pltpu.VMEM((2, LANES // 2, 512), f32),
            pltpu.VMEM((2, DEVICES, 256), f32),
            pltpu.VMEM((2, 256, LANES), f32),
            pltpu.VMEM((DEVICES - 1, 4, LANES), f32),
            pltpu.SemaphoreType.DMA((len(CHUNKS) + 5,)),
            pltpu.SemaphoreType.DMA((COLS, 2)),
            pltpu.SemaphoreType.DMA((COLS, 2)),
            pltpu.SemaphoreType.DMA((2, 2)),
            pltpu.SemaphoreType.DMA((COLS, 2)),
            pltpu.SemaphoreType.DMA,
            pltpu.SemaphoreType.DMA,
            pltpu.SemaphoreType.REGULAR,
            pltpu.SemaphoreType.REGULAR,
        ],
        compiler_params=pltpu.CompilerParams(
            collective_id=0, has_side_effects=True, vmem_limit_bytes=54936 * 2**10
        ),
    )(field, *[jnp.asarray(c) for c in constants])
    return power[None]


def solution(mesh):
    return jax.shard_map(
        local,
        mesh=mesh,
        in_specs=(P(None, "rows", "cols"),),
        out_specs=P(None, ("rows", "cols"), None),
        check_vma=False,
    )
```

```python
import jax
import jax.numpy as jnp
import ml_dtypes
import numpy as np
from jax import lax
from jax.experimental import pallas as pl
from jax.experimental.pallas import tpu as pltpu
from jax.sharding import PartitionSpec as P

TAPS = 33
STRIDE = 8
REACH = TAPS // 2
MESH = pl.DeviceIdType.MESH

ROWS, COLS = 32, 4
DEVICES = ROWS * COLS
LENGTH = 2304
RADIX = LENGTH // DEVICES
RAW_ROWS = LENGTH * STRIDE // ROWS
RAW_COLS = LENGTH * STRIDE // COLS
OUT_COLS = RAW_COLS // STRIDE
CORES = 2
HOLD = CORES * RADIX
SLOT = 40
BLOCK = CORES * SLOT
PAIRS = DEVICES // CORES
LANES = 128
WIDE = 5 * LANES
HALF = RADIX // 2


FARTHEST = 74
NEARNESS = 2


def bend(place):
    return (place & 1) + 2 * ((place >> 1) & (1 - (place & 1)))


def hops(device):
    y = (device & 2) + ((device >> 4) & 1)
    return bend((device >> 2) & 3) + bend((device >> 5) & 3) + bend(y)


NEAR_ORIGIN = sorted((d for d in range(DEVICES) if hops(d) <= NEARNESS), key=hops)
GROUP_B = [4 * k for k in range(1, 8)]
GROUP_C = [low + 32 * z for z in (2, 1, 3, 0) for low in (2, 3, 0, 1) if low or z]
CUTS = [0] + [LANES + 1024 * t for t in range(5)] + [RAW_COLS]
CHUNKS = list(zip(CUTS[:-1], CUTS[1:]))


def taps_table():
    tap_ids = np.arange(TAPS, dtype=np.float32)
    shaped = np.sinc((tap_ids - np.float32(REACH)) / np.float32(STRIDE)).astype(np.float32)
    shaped = shaped * (
        np.float32(0.54)
        - np.float32(0.46) * np.cos(np.float32(2 * np.pi) * tap_ids / np.float32(TAPS - 1))
    )
    shaped = shaped / np.sum(shaped)
    return shaped.astype(ml_dtypes.bfloat16).astype(np.float32)


def tap_at(offset):
    taps = taps_table()
    inside = (offset >= 0) & (offset < TAPS)
    return np.where(inside, taps[np.clip(offset, 0, TAPS - 1)], 0).astype(ml_dtypes.bfloat16)


def split(matrix):
    high = matrix.astype(ml_dtypes.bfloat16)
    low = (matrix - high.astype(np.float64)).astype(ml_dtypes.bfloat16)
    return high, low


def tables():
    own = np.full((CORES, SLOT), -(10**6))
    own[:, :HOLD] = HOLD * np.arange(CORES)[:, None] + np.arange(HOLD)
    own[0, HOLD : HOLD + 2] = [-2, -1]
    own[1, HOLD : HOLD + 2] = [CORES * HOLD, CORES * HOLD + 1]
    raw = np.arange(RAW_ROWS)
    row_band = tap_at(raw[None, :] - STRIDE * own.reshape(-1, 1) + REACH)
    row_band = np.pad(row_band, ((0, 192 - BLOCK), (0, WIDE - RAW_ROWS)))

    lane = np.arange(LANES)
    inner = tap_at(np.arange(10 * LANES)[:, None] - LANES - STRIDE * lane[None, :] + REACH)
    edge = tap_at(lane[:, None] - STRIDE * (lane[None, :] - LANES) + REACH)
    col_band = np.concatenate([inner, edge], axis=0)

    def wave(places, count):
        angle = 2 * np.pi / LANES * (places[:, None] * np.arange(count)[None, :] % LANES)
        cos, sin = np.cos(angle), np.sin(angle)
        return np.block([[cos, -sin], [sin, cos]])

    pair = np.arange(PAIRS)
    first = np.concatenate(split(wave(lane, LANES // 2).T), axis=1)
    main = np.concatenate([wave(2 * pair + e, LANES) for e in range(2)], axis=1)
    odd = np.tile(pair % 2, 2)[:, None]
    before = wave(2 * pair - 1, LANES) * (1 - odd)
    after = wave(2 * pair + 2, LANES) * odd
    main_high, main_low = split(main)
    edge_high, edge_low = split(np.concatenate([before, after], axis=1))
    matrices = np.concatenate(
        [first, main_high, main_high, main_low, edge_high, edge_high, edge_low], axis=0
    )

    window = 0.5 - 0.5 * np.cos(2 * np.pi * np.arange(LENGTH) / LENGTH)
    held = own[pair % 2] + (HOLD * CORES) * (pair[:, None] // 2)
    inside = (held >= 0) & (held < LENGTH)
    row_window = np.where(inside, window[np.clip(held, 0, LENGTH - 1)], 0)
    row_window = np.broadcast_to(row_window.reshape(-1, 1), (PAIRS * SLOT, LANES))

    turn = 2 * np.pi / LENGTH * (np.arange(RADIX)[:, None] * lane[None, :])
    later = np.pad(np.stack([np.cos(turn), np.sin(turn)]), ((0, 0), (0, 24 - RADIX), (0, 0)))
    side_tables = []
    for side in range(2):
        sign = np.where(side * np.arange(24) % 2, -1.0, 1.0)[None, :, None]
        start = HALF * LANES * side
        block = window[start : start + HALF * LANES].reshape(HALF, LANES)
        weights = np.zeros((12, LANES))
        weights[:9] = block
        weights[4] = np.where(lane < 66, block[4], 0)
        weights[9] = np.where(lane >= 62, block[4], 0)
        if side == 0:
            weights[10, :2] = window[HALF * LANES : HALF * LANES + 2]
        else:
            weights[11, -2:] = window[HALF * LANES - 2 : HALF * LANES]
        weights = np.repeat(weights, 8, axis=0)
        side_tables.append((later * sign).reshape(-1, LANES))
        side_tables += [later.reshape(-1, LANES), weights]
    floats = np.concatenate([row_window] + side_tables, axis=0)
    return row_band, col_band, matrices, floats.astype(np.float32)


def real_nine(points):
    sums = [points[m] + points[9 - m] for m in range(1, 5)]
    gaps = [points[m] - points[9 - m] for m in range(1, 5)]
    reals, imags = [points[0] + sums[0] + sums[1] + sums[2] + sums[3]], [None]
    for freq in range(1, 5):
        real, imag = points[0], None
        for m in range(1, 5):
            phase = 2 * np.pi * (m * freq % 9) / 9
            real = real + sums[m - 1] * np.float32(np.cos(phase))
            term = gaps[m - 1] * np.float32(-np.sin(phase))
            imag = term if imag is None else imag + term
        reals.append(real)
        imags.append(imag)
    return reals, imags


def folded(points):
    evens = [points[2 * b % 18] for b in range(9)]
    odds = [points[(9 + 2 * b) % 18] for b in range(9)]
    sums, gaps = [], []
    for even, odd in zip(evens, odds):
        if odd is None:
            sums.append(even)
            gaps.append(even)
        elif even is None:
            sums.append(odd)
            gaps.append(-odd)
        else:
            sums.append(even + odd)
            gaps.append(even - odd)
    return real_nine(sums), real_nine(gaps)


def real_eighteen(points):
    both = folded(points)
    out = []
    for freq in range(18):
        reals, imags = both[freq % 2]
        at = freq % 9
        if at == 0:
            out.append((reals[0], None))
        elif at <= 4:
            out.append((reals[at], imags[at]))
        else:
            out.append((reals[9 - at], -imags[9 - at]))
    return out


def complex_eighteen(real_points, imag_points):
    both_real, both_imag = folded(real_points), folded(imag_points)
    out = []
    for freq in range(18):
        (a_re, a_im), (b_re, b_im) = both_real[freq % 2], both_imag[freq % 2]
        at = freq % 9
        if at == 0:
            out.append((a_re[0], b_re[0]))
        elif at <= 4:
            out.append((a_re[at] - b_im[at], a_im[at] + b_re[at]))
        else:
            out.append((a_re[9 - at] + b_im[9 - at], b_re[9 - at] - a_im[9 - at]))
    return out


def halves(value):
    high = value.astype(jnp.bfloat16)
    low = (value - high.astype(jnp.float32)).astype(jnp.bfloat16)
    return high, low


def product(left, right, dims):
    return lax.dot_general(left, right, (dims, ((), ())), preferred_element_type=jnp.float32)


def kernel(
    field, row_band_in, col_band_in, matrices_in, floats_in,
    power,
    raw, row_band, col_band, matrices, common, row_window,
    rowcut, cut, gathered, turned, leaving, arrived, mixed, beyond, filler,
    load_sem, near_send, near_recv, far_send, far_recv, all_ready,
):
    p, q = lax.axis_index("rows"), lax.axis_index("cols")
    me = p * COLS + q
    side, core = q >> 1, q & 1
    pair = p * CORES + core
    def peer(k):
        return (p ^ (k >> 2), q ^ (k & 3))

    small = len(CHUNKS)
    loads = [
        pltpu.make_async_copy(row_band_in.at[pl.ds(0, BLOCK)], row_band, load_sem.at[small]),
        pltpu.make_async_copy(col_band_in, col_band, load_sem.at[small + 1]),
        pltpu.make_async_copy(matrices_in, matrices, load_sem.at[small + 2]),
        pltpu.make_async_copy(
            floats_in.at[pl.ds(pl.multiple_of(pair * SLOT, 8), SLOT)],
            row_window,
            load_sem.at[small + 3],
        ),
        pltpu.make_async_copy(
            floats_in.at[pl.ds(pl.multiple_of(PAIRS * SLOT + side * 192, 8), 192)],
            common,
            load_sem.at[small + 4],
        ),
    ]
    field_loads = [
        pltpu.make_async_copy(
            field.at[0, :, pl.ds(lo, hi - lo)], raw.at[:, pl.ds(lo, hi - lo)], load_sem.at[t]
        )
        for t, (lo, hi) in enumerate(CHUNKS)
    ]
    for copy in loads[:1] + field_loads[:2] + loads[1:2]:
        copy.start()

    def signal(semaphore, device):
        pl.semaphore_signal(semaphore, inc=1, device_id=device, device_id_type=MESH)

    barrier = pltpu.get_barrier_semaphore()
    for k in GROUP_C + GROUP_B:
        signal(barrier, peer(k))
    for copy in field_loads[2:] + loads[2:]:
        copy.start()

    for row in (360, 384 + 360):
        turned[pl.ds(row, 24), :] = jnp.zeros((24, 256), jnp.float32)

    def row_copy(part, lo, size):
        to = 1 - core
        return pltpu.make_async_remote_copy(
            src_ref=cut.at[pl.ds(pl.multiple_of(to * SLOT, 8), SLOT), pl.ds(lo, size)],
            dst_ref=gathered.at[core, :, pl.ds(lo, size)],
            send_sem=near_send.at[part],
            recv_sem=near_recv.at[part],
            device_id=(p, q ^ 1),
            device_id_type=MESH,
        )

    near = [row_copy(0, 0, 4 * LANES), row_copy(1, 4 * LANES, LANES)]

    def filter_rows(begin, size):
        part = product(row_band[:, :RAW_ROWS], raw[:, pl.ds(begin, size)], ((1,), (0,)))
        high, low = halves(part)
        rowcut[: BLOCK, pl.ds(begin + LANES, size)] = high
        rowcut[BLOCK :, pl.ds(begin + LANES, size)] = low

    rowcut[:, :LANES] = jnp.zeros((2 * BLOCK, LANES), jnp.bfloat16)
    loads[0].wait()
    field_loads[0].wait()
    filter_rows(0, LANES)
    loads[1].wait()

    def step(u):
        begin = pl.multiple_of(1024 * u, LANES)
        chunk = raw.at[:, pl.ds(begin + LANES, 1024)]
        pltpu.make_async_copy(chunk, chunk, load_sem.at[u + 1]).wait()
        filter_rows(begin + LANES, 1024)
        both = product(
            rowcut[:, pl.ds(begin, 10 * LANES)], col_band[: 10 * LANES, :], ((1,), (0,))
        )
        cut[:, pl.ds(pl.multiple_of(LANES * u, LANES), LANES)] = (
            both[: BLOCK] + both[BLOCK :]
        )

    pl.loop(0, 3)(step)
    pl.semaphore_wait(barrier, len(GROUP_B + GROUP_C))
    for k in GROUP_B:
        signal(all_ready, peer(k))
    pl.loop(3, 4)(step)
    near[0].start()
    field_loads[5].wait()
    filter_rows(CUTS[5], RAW_COLS - CUTS[5])
    both = product(
        rowcut[:, 4096 : RAW_COLS + LANES], col_band[: RAW_COLS + LANES - 4096, :], ((1,), (0,))
    ) + product(rowcut[:, LANES : 2 * LANES], col_band[10 * LANES :, :], ((1,), (0,)))
    cut[:, 4 * LANES :] = both[: BLOCK] + both[BLOCK :]
    near[1].start()
    gathered[core] = cut[pl.ds(pl.multiple_of(core * SLOT, 8), SLOT), :]
    for copy in loads[2:]:
        copy.wait()
    for copy in near:
        copy.wait_recv()

    @pl.loop(0, SLOT // 8)
    def _(s):
        rows = pl.ds(pl.multiple_of(8 * s, 8), 8)
        mine = row_window[rows, :]
        left, right = gathered[0, rows, :], pltpu.roll(gathered[1, rows, :], 64, 1)

        def weighted(block, t, at):
            weight = common[96 + 8 * at : 104 + 8 * at, :]
            return block[:, LANES * t : LANES * (t + 1)] * mine * weight

        points = [None] * RADIX
        for t in range(4):
            points[t] = weighted(left, t, t)
            points[5 + t] = weighted(right, 1 + t, 5 + t)
        points[4] = weighted(left, 4, 4) + weighted(right, 0, 9)
        points[9] = weighted(right, 0, 10)
        points[17] = weighted(left, 4, 11)
        for freq, (real, imag) in enumerate(real_eighteen(points)):
            half, low = divmod(freq, HALF)
            at = 384 * half + jnp.where(s < 4, 32 * low + 8 * s, 288 + 8 * low)
            out = pl.ds(pl.multiple_of(at, 8), 8)
            cos, sin = common[freq : freq + 1, :], common[24 + freq : 25 + freq, :]
            if imag is None:
                turned[out, :LANES] = real * cos
                turned[out, LANES:] = -real * sin
            else:
                turned[out, :LANES] = real * cos + imag * sin
                turned[out, LANES:] = imag * cos - real * sin

    first_high, first_low = matrices[:LANES, :256], matrices[:LANES, 256:]

    @pl.loop(0, 2)
    def _(h):
        part = pl.ds(pl.multiple_of(384 * h, LANES), 384)
        high, low = halves(turned[part, :])
        both = (
            product(first_high, low, ((1,), (1,)))
            + product(first_low, high, ((1,), (1,)))
            + product(first_high, high, ((1,), (1,)))
        )
        leaving[0, :, part] = both[: LANES // 2]
        leaving[1, :, part] = both[LANES // 2 :]

    def block_of(other):
        lanes = pl.multiple_of((other & 1) * 384, LANES)
        return leaving.at[:, pl.ds(other >> 1, 1), pl.ds(lanes, 384)]

    landing = arrived.at[side, :, pl.ds(pair, 1), :]

    pl.semaphore_wait(all_ready, len(GROUP_B))
    def far(other):
        pltpu.make_async_remote_copy(
            src_ref=block_of(other),
            dst_ref=landing,
            send_sem=far_send,
            recv_sem=far_recv,
            device_id=(other >> 2, other & 3),
            device_id_type=MESH,
        ).start()

    for first in NEAR_ORIGIN:

        @pl.when(me != first)
        def _():
            far(jnp.int32(first))

    @pl.loop(0, DEVICES)
    def _(step):
        other = me ^ step ^ FARTHEST

        @pl.when((hops(other) > NEARNESS) & (other != me))
        def _():
            far(other)

    pltpu.make_async_copy(block_of(me), landing, far_recv).start()
    pltpu.make_async_copy(arrived, arrived, far_recv).wait()

    high, low = halves((arrived[0] + arrived[1]).reshape(2 * PAIRS, 384).T)
    both = jnp.concatenate([high, low], axis=1)
    total = product(both, matrices[128:384, :], ((1,), (0,))) + product(
        high, matrices[384:512, :], ((1,), (0,))
    )
    rest = product(both[288:360], matrices[512:768, :], ((1,), (0,))) + product(
        high[288:360], matrices[768:896, :], ((1,), (0,))
    )
    for t in range(4):
        mixed[t] = total[:, LANES * t : LANES * (t + 1)]
        beyond[t] = rest[:, LANES * t : LANES * (t + 1)]

    def held(e, part, slot):
        if slot < 32:
            return mixed[2 * e + part, pl.ds(slot, HALF, stride=32), :]
        return mixed[2 * e + part, pl.ds(288 + slot - 32, HALF, stride=8), :]

    real_points, imag_points = [], []
    for r in range(RADIX):
        real, imag = (held(0, part, r) + held(1, part, RADIX + r) for part in range(2))
        if r < 2:
            real = real + beyond[2, pl.ds(4 + r, HALF, stride=8), :]
            imag = imag + beyond[3, pl.ds(4 + r, HALF, stride=8), :]
        if r >= RADIX - 2:
            real = real + beyond[0, pl.ds(4 + r - (RADIX - 2), HALF, stride=8), :]
            imag = imag + beyond[1, pl.ds(4 + r - (RADIX - 2), HALF, stride=8), :]
        cos, sin = common[48 + r : 49 + r, :], common[72 + r : 73 + r, :]
        real_points.append(real * cos + imag * sin)
        imag_points.append(imag * cos - real * sin)
    for freq, (real, imag) in enumerate(complex_eighteen(real_points, imag_points)):
        power[:, LANES * freq : LANES * (freq + 1)] = (real * real + imag * imag) * np.float32(
            8.0 / (LENGTH * LENGTH)
        )

    for copy in near:
        copy.wait_send()
    pltpu.make_async_copy(filler, filler, far_send).wait()


def local(field):
    constants = tables()
    anywhere = pl.BlockSpec(memory_space=pltpu.HBM)
    f32, bf16 = jnp.float32, jnp.bfloat16
    power = pl.pallas_call(
        kernel,
        out_shape=jax.ShapeDtypeStruct((HALF, LENGTH), f32),
        in_specs=[anywhere] * (1 + len(constants)),
        out_specs=pl.BlockSpec(memory_space=pltpu.VMEM),
        scratch_shapes=[
            pltpu.VMEM((RAW_ROWS, RAW_COLS), bf16),
            pltpu.VMEM((BLOCK, WIDE), bf16),
            pltpu.VMEM(constants[1].shape, bf16),
            pltpu.VMEM(constants[2].shape, bf16),
            pltpu.VMEM((192, LANES), f32),
            pltpu.VMEM((SLOT, LANES), f32),
            pltpu.VMEM((2 * BLOCK, RAW_COLS + LANES), bf16),
            pltpu.VMEM((BLOCK, WIDE), f32),
            pltpu.VMEM((CORES, SLOT, WIDE), f32),
            pltpu.VMEM((768, 256), f32),
            pltpu.VMEM((2, LANES // 2, 768), f32),
            pltpu.VMEM((2, 2, PAIRS, 384), f32),
            pltpu.VMEM((4, 384, LANES), f32),
            pltpu.VMEM((4, 72, LANES), f32),
            pltpu.VMEM((DEVICES - 1, 6, LANES), f32),
            pltpu.SemaphoreType.DMA((len(CHUNKS) + 5,)),
            pltpu.SemaphoreType.DMA((2,)),
            pltpu.SemaphoreType.DMA((2,)),
            pltpu.SemaphoreType.DMA,
            pltpu.SemaphoreType.DMA,
            pltpu.SemaphoreType.REGULAR,
        ],
        compiler_params=pltpu.CompilerParams(
            collective_id=0, has_side_effects=True, vmem_limit_bytes=54936 * 2**10
        ),
    )(field, *[jnp.asarray(c) for c in constants])
    return power[None]


def solution(mesh):
    return jax.shard_map(
        local,
        mesh=mesh,
        in_specs=(P(None, "rows", "cols"),),
        out_specs=P(None, ("rows", "cols"), None),
        check_vma=False,
    )
```

```python
import jax
import jax.numpy as jnp
import ml_dtypes
import numpy as np
from jax import lax
from jax.experimental import pallas as pl
from jax.experimental.pallas import tpu as pltpu
from jax.sharding import PartitionSpec as P

TAPS = 33
STRIDE = 8
REACH = TAPS // 2
MESH = pl.DeviceIdType.MESH

ROWS, COLS = 32, 4
DEVICES = ROWS * COLS
LENGTH = 2304
RADIX = LENGTH // DEVICES
RAW_ROWS = LENGTH * STRIDE // ROWS
RAW_COLS = LENGTH * STRIDE // COLS
OUT_COLS = RAW_COLS // STRIDE
CORES = 2
HOLD = CORES * RADIX
SLOT = 40
BLOCK = CORES * SLOT
PAIRS = DEVICES // CORES
LANES = 128
WIDE = 5 * LANES
HALF = RADIX // 2


FARTHEST = 74
NEARNESS = 2


def bend(place):
    return (place & 1) + 2 * ((place >> 1) & (1 - (place & 1)))


def hops(device):
    y = (device & 2) + ((device >> 4) & 1)
    return bend((device >> 2) & 3) + bend((device >> 5) & 3) + bend(y)


NEAR_ORIGIN = sorted((d for d in range(DEVICES) if hops(d) <= NEARNESS), key=hops)
GROUP_B = [4 * k for k in range(1, 8)]
GROUP_C = [low + 32 * z for z in (2, 1, 3, 0) for low in (2, 3, 0, 1) if low or z]
CUTS = [0] + [LANES + 1024 * t for t in range(5)] + [RAW_COLS]
CHUNKS = list(zip(CUTS[:-1], CUTS[1:]))


def taps_table():
    tap_ids = np.arange(TAPS, dtype=np.float32)
    shaped = np.sinc((tap_ids - np.float32(REACH)) / np.float32(STRIDE)).astype(np.float32)
    shaped = shaped * (
        np.float32(0.54)
        - np.float32(0.46) * np.cos(np.float32(2 * np.pi) * tap_ids / np.float32(TAPS - 1))
    )
    shaped = shaped / np.sum(shaped)
    return shaped.astype(ml_dtypes.bfloat16).astype(np.float32)


def tap_at(offset):
    taps = taps_table()
    inside = (offset >= 0) & (offset < TAPS)
    return np.where(inside, taps[np.clip(offset, 0, TAPS - 1)], 0).astype(ml_dtypes.bfloat16)


def split(matrix):
    high = matrix.astype(ml_dtypes.bfloat16)
    low = (matrix - high.astype(np.float64)).astype(ml_dtypes.bfloat16)
    return high, low


def tables():
    own = np.full((CORES, SLOT), -(10**6))
    own[:, :HOLD] = HOLD * np.arange(CORES)[:, None] + np.arange(HOLD)
    own[0, HOLD : HOLD + 2] = [-2, -1]
    own[1, HOLD : HOLD + 2] = [CORES * HOLD, CORES * HOLD + 1]
    raw = np.arange(RAW_ROWS)
    row_band = tap_at(raw[None, :] - STRIDE * own.reshape(-1, 1) + REACH)
    row_band = np.pad(row_band, ((0, 192 - BLOCK), (0, WIDE - RAW_ROWS)))

    lane = np.arange(LANES)
    inner = tap_at(np.arange(10 * LANES)[:, None] - LANES - STRIDE * lane[None, :] + REACH)
    edge = tap_at(lane[:, None] - STRIDE * (lane[None, :] - LANES) + REACH)
    col_band = np.concatenate([inner, edge], axis=0)

    def wave(places, count):
        angle = 2 * np.pi / LANES * (places[:, None] * np.arange(count)[None, :] % LANES)
        cos, sin = np.cos(angle), np.sin(angle)
        return np.block([[cos, -sin], [sin, cos]])

    pair = np.arange(PAIRS)
    first = np.concatenate(split(wave(lane, LANES // 2).T), axis=1)
    main = np.concatenate([wave(2 * pair + e, LANES) for e in range(2)], axis=1)
    odd = np.tile(pair % 2, 2)[:, None]
    before = wave(2 * pair - 1, LANES) * (1 - odd)
    after = wave(2 * pair + 2, LANES) * odd
    main_high, main_low = split(main)
    edge_high, edge_low = split(np.concatenate([before, after], axis=1))
    matrices = np.concatenate(
        [first, main_high, main_high, main_low, edge_high, edge_high, edge_low], axis=0
    )

    window = 0.5 - 0.5 * np.cos(2 * np.pi * np.arange(LENGTH) / LENGTH)
    held = own[pair % 2] + (HOLD * CORES) * (pair[:, None] // 2)
    inside = (held >= 0) & (held < LENGTH)
    row_window = np.where(inside, window[np.clip(held, 0, LENGTH - 1)], 0)
    row_window = np.broadcast_to(row_window.reshape(-1, 1), (PAIRS * SLOT, LANES))

    turn = 2 * np.pi / LENGTH * (np.arange(RADIX)[:, None] * lane[None, :])
    later = np.pad(np.stack([np.cos(turn), np.sin(turn)]), ((0, 0), (0, 24 - RADIX), (0, 0)))
    side_tables = []
    for side in range(2):
        sign = np.where(side * np.arange(24) % 2, -1.0, 1.0)[None, :, None]
        start = HALF * LANES * side
        block = window[start : start + HALF * LANES].reshape(HALF, LANES)
        weights = np.zeros((12, LANES))
        weights[:9] = block
        weights[4] = np.where(lane < 66, block[4], 0)
        weights[9] = np.where(lane >= 62, block[4], 0)
        if side == 0:
            weights[10, :2] = window[HALF * LANES : HALF * LANES + 2]
        else:
            weights[11, -2:] = window[HALF * LANES - 2 : HALF * LANES]
        weights = np.repeat(weights, 8, axis=0)
        side_tables.append((later * sign).reshape(-1, LANES))
        side_tables += [later.reshape(-1, LANES), weights]
    floats = np.concatenate([row_window] + side_tables, axis=0)
    return row_band, col_band, matrices, floats.astype(np.float32)


def real_nine(points):
    sums = [points[m] + points[9 - m] for m in range(1, 5)]
    gaps = [points[m] - points[9 - m] for m in range(1, 5)]
    reals, imags = [points[0] + sums[0] + sums[1] + sums[2] + sums[3]], [None]
    for freq in range(1, 5):
        real, imag = points[0], None
        for m in range(1, 5):
            phase = 2 * np.pi * (m * freq % 9) / 9
            real = real + sums[m - 1] * np.float32(np.cos(phase))
            term = gaps[m - 1] * np.float32(-np.sin(phase))
            imag = term if imag is None else imag + term
        reals.append(real)
        imags.append(imag)
    return reals, imags


def folded(points):
    evens = [points[2 * b % 18] for b in range(9)]
    odds = [points[(9 + 2 * b) % 18] for b in range(9)]
    sums, gaps = [], []
    for even, odd in zip(evens, odds):
        if odd is None:
            sums.append(even)
            gaps.append(even)
        elif even is None:
            sums.append(odd)
            gaps.append(-odd)
        else:
            sums.append(even + odd)
            gaps.append(even - odd)
    return real_nine(sums), real_nine(gaps)


def real_eighteen(points):
    both = folded(points)
    out = []
    for freq in range(18):
        reals, imags = both[freq % 2]
        at = freq % 9
        if at == 0:
            out.append((reals[0], None))
        elif at <= 4:
            out.append((reals[at], imags[at]))
        else:
            out.append((reals[9 - at], -imags[9 - at]))
    return out


def complex_eighteen(real_points, imag_points):
    both_real, both_imag = folded(real_points), folded(imag_points)
    out = []
    for freq in range(18):
        (a_re, a_im), (b_re, b_im) = both_real[freq % 2], both_imag[freq % 2]
        at = freq % 9
        if at == 0:
            out.append((a_re[0], b_re[0]))
        elif at <= 4:
            out.append((a_re[at] - b_im[at], a_im[at] + b_re[at]))
        else:
            out.append((a_re[9 - at] + b_im[9 - at], b_re[9 - at] - a_im[9 - at]))
    return out


def halves(value):
    high = value.astype(jnp.bfloat16)
    low = (value - high.astype(jnp.float32)).astype(jnp.bfloat16)
    return high, low


def product(left, right, dims):
    return lax.dot_general(left, right, (dims, ((), ())), preferred_element_type=jnp.float32)


def kernel(
    field, row_band_in, col_band_in, matrices_in, floats_in,
    power,
    raw, row_band, col_band, matrices, common, row_window,
    rowcut, cut, gathered, turned, leaving, arrived, mixed, beyond, filler,
    load_sem, near_send, near_recv, far_send, far_recv, all_ready,
):
    p, q = lax.axis_index("rows"), lax.axis_index("cols")
    me = p * COLS + q
    side, core = q >> 1, q & 1
    pair = p * CORES + core
    def peer(k):
        return (p ^ (k >> 2), q ^ (k & 3))

    small = len(CHUNKS)
    loads = [
        pltpu.make_async_copy(row_band_in.at[pl.ds(0, BLOCK)], row_band, load_sem.at[small]),
        pltpu.make_async_copy(col_band_in, col_band, load_sem.at[small + 1]),
        pltpu.make_async_copy(matrices_in, matrices, load_sem.at[small + 2]),
        pltpu.make_async_copy(
            floats_in.at[pl.ds(pl.multiple_of(pair * SLOT, 8), SLOT)],
            row_window,
            load_sem.at[small + 3],
        ),
        pltpu.make_async_copy(
            floats_in.at[pl.ds(pl.multiple_of(PAIRS * SLOT + side * 192, 8), 192)],
            common,
            load_sem.at[small + 4],
        ),
    ]
    field_loads = [
        pltpu.make_async_copy(
            field.at[0, :, pl.ds(lo, hi - lo)], raw.at[:, pl.ds(lo, hi - lo)], load_sem.at[t]
        )
        for t, (lo, hi) in enumerate(CHUNKS)
    ]
    for copy in loads[:1] + field_loads[:2] + loads[1:2] + field_loads[2:]:
        copy.start()

    def signal(semaphore, device):
        pl.semaphore_signal(semaphore, inc=1, device_id=device, device_id_type=MESH)

    barrier = pltpu.get_barrier_semaphore()
    for k in GROUP_C + GROUP_B:
        signal(barrier, peer(k))

    for row in (360, 384 + 360):
        turned[pl.ds(row, 24), :] = jnp.zeros((24, 256), jnp.float32)

    def row_copy(part, lo, size):
        to = 1 - core
        return pltpu.make_async_remote_copy(
            src_ref=cut.at[pl.ds(pl.multiple_of(to * SLOT, 8), SLOT), pl.ds(lo, size)],
            dst_ref=gathered.at[core, :, pl.ds(lo, size)],
            send_sem=near_send.at[part],
            recv_sem=near_recv.at[part],
            device_id=(p, q ^ 1),
            device_id_type=MESH,
        )

    near = [row_copy(0, 0, 4 * LANES), row_copy(1, 4 * LANES, LANES)]

    def filter_rows(begin, size):
        part = product(row_band[:, :RAW_ROWS], raw[:, pl.ds(begin, size)], ((1,), (0,)))
        high, low = halves(part)
        rowcut[: BLOCK, pl.ds(begin + LANES, size)] = high
        rowcut[BLOCK :, pl.ds(begin + LANES, size)] = low

    rowcut[:, :LANES] = jnp.zeros((2 * BLOCK, LANES), jnp.bfloat16)
    loads[0].wait()
    field_loads[0].wait()
    filter_rows(0, LANES)
    loads[1].wait()

    def step(u):
        begin = pl.multiple_of(1024 * u, LANES)
        chunk = raw.at[:, pl.ds(begin + LANES, 1024)]
        pltpu.make_async_copy(chunk, chunk, load_sem.at[u + 1]).wait()
        filter_rows(begin + LANES, 1024)
        both = product(
            rowcut[:, pl.ds(begin, 10 * LANES)], col_band[: 10 * LANES, :], ((1,), (0,))
        )
        cut[:, pl.ds(pl.multiple_of(LANES * u, LANES), LANES)] = (
            both[: BLOCK] + both[BLOCK :]
        )

    pl.loop(0, 3)(step)
    for copy in loads[2:]:
        copy.start()
    pl.semaphore_wait(barrier, len(GROUP_B + GROUP_C))
    for k in GROUP_B:
        signal(all_ready, peer(k))
    pl.loop(3, 4)(step)
    near[0].start()
    field_loads[5].wait()
    filter_rows(CUTS[5], RAW_COLS - CUTS[5])
    both = product(
        rowcut[:, 4096 : RAW_COLS + LANES], col_band[: RAW_COLS + LANES - 4096, :], ((1,), (0,))
    ) + product(rowcut[:, LANES : 2 * LANES], col_band[10 * LANES :, :], ((1,), (0,)))
    cut[:, 4 * LANES :] = both[: BLOCK] + both[BLOCK :]
    near[1].start()
    gathered[core] = cut[pl.ds(pl.multiple_of(core * SLOT, 8), SLOT), :]
    for copy in loads[2:]:
        copy.wait()
    for copy in near:
        copy.wait_recv()

    @pl.loop(0, SLOT // 8)
    def _(s):
        rows = pl.ds(pl.multiple_of(8 * s, 8), 8)
        mine = row_window[rows, :]
        left, right = gathered[0, rows, :], pltpu.roll(gathered[1, rows, :], 64, 1)

        def weighted(block, t, at):
            weight = common[96 + 8 * at : 104 + 8 * at, :]
            return block[:, LANES * t : LANES * (t + 1)] * mine * weight

        points = [None] * RADIX
        for t in range(4):
            points[t] = weighted(left, t, t)
            points[5 + t] = weighted(right, 1 + t, 5 + t)
        points[4] = weighted(left, 4, 4) + weighted(right, 0, 9)
        points[9] = weighted(right, 0, 10)
        points[17] = weighted(left, 4, 11)
        for freq, (real, imag) in enumerate(real_eighteen(points)):
            half, low = divmod(freq, HALF)
            out = pl.ds(pl.multiple_of(384 * half + 72 * s + 8 * low, 8), 8)
            cos, sin = common[freq : freq + 1, :], common[24 + freq : 25 + freq, :]
            if imag is None:
                turned[out, :LANES] = real * cos
                turned[out, LANES:] = -real * sin
            else:
                turned[out, :LANES] = real * cos + imag * sin
                turned[out, LANES:] = imag * cos - real * sin

    first_high, first_low = matrices[:LANES, :256], matrices[:LANES, 256:]

    @pl.loop(0, 2)
    def _(h):
        part = pl.ds(pl.multiple_of(384 * h, LANES), 384)
        high, low = halves(turned[part, :])
        both = (
            product(first_high, low, ((1,), (1,)))
            + product(first_low, high, ((1,), (1,)))
            + product(first_high, high, ((1,), (1,)))
        )
        leaving[0, :, part] = both[: LANES // 2]
        leaving[1, :, part] = both[LANES // 2 :]

    def block_of(other):
        lanes = pl.multiple_of((other & 1) * 384, LANES)
        return leaving.at[:, pl.ds(other >> 1, 1), pl.ds(lanes, 384)]

    landing = arrived.at[side, :, pl.ds(pair, 1), :]

    pl.semaphore_wait(all_ready, len(GROUP_B))

    def far(other):
        pltpu.make_async_remote_copy(
            src_ref=block_of(other),
            dst_ref=landing,
            send_sem=far_send,
            recv_sem=far_recv,
            device_id=(other >> 2, other & 3),
            device_id_type=MESH,
        ).start()

    for first in NEAR_ORIGIN:

        @pl.when(me != first)
        def _():
            far(jnp.int32(first))

    @pl.loop(0, DEVICES)
    def _(step):
        other = me ^ step ^ FARTHEST

        @pl.when((hops(other) > NEARNESS) & (other != me))
        def _():
            far(other)

    pltpu.make_async_copy(block_of(me), landing, far_recv).start()
    pltpu.make_async_copy(arrived, arrived, far_recv).wait()

    high, low = halves((arrived[0] + arrived[1]).reshape(2 * PAIRS, 384).T)
    both = jnp.concatenate([high, low], axis=1)
    for e in range(2):
        rows, lanes = slice(144 * e, 144 * e + 216), slice(256 * e, 256 * e + 256)
        total = product(both[rows], matrices[128:384, lanes], ((1,), (0,))) + product(
            high[rows], matrices[384:512, lanes], ((1,), (0,))
        )
        mixed[2 * e], mixed[2 * e + 1] = total[:, :LANES], total[:, LANES:]
    rest = product(both[288:360], matrices[512:768, :], ((1,), (0,))) + product(
        high[288:360], matrices[768:896, :], ((1,), (0,))
    )
    for t in range(4):
        beyond[t] = rest[:, LANES * t : LANES * (t + 1)]

    def held(e, part, slot):
        row = 72 * (slot // 8) + slot % 8 - 144 * e
        return mixed[2 * e + part, pl.ds(row, HALF, stride=8), :]

    real_points, imag_points = [], []
    for r in range(RADIX):
        real, imag = (held(0, part, r) + held(1, part, RADIX + r) for part in range(2))
        if r < 2:
            real = real + beyond[2, pl.ds(4 + r, HALF, stride=8), :]
            imag = imag + beyond[3, pl.ds(4 + r, HALF, stride=8), :]
        if r >= RADIX - 2:
            real = real + beyond[0, pl.ds(4 + r - (RADIX - 2), HALF, stride=8), :]
            imag = imag + beyond[1, pl.ds(4 + r - (RADIX - 2), HALF, stride=8), :]
        cos, sin = common[48 + r : 49 + r, :], common[72 + r : 73 + r, :]
        real_points.append(real * cos + imag * sin)
        imag_points.append(imag * cos - real * sin)
    for freq, (real, imag) in enumerate(complex_eighteen(real_points, imag_points)):
        power[:, LANES * freq : LANES * (freq + 1)] = (real * real + imag * imag) * np.float32(
            8.0 / (LENGTH * LENGTH)
        )

    for copy in near:
        copy.wait_send()
    pltpu.make_async_copy(filler, filler, far_send).wait()


def local(field):
    constants = tables()
    anywhere = pl.BlockSpec(memory_space=pltpu.HBM)
    f32, bf16 = jnp.float32, jnp.bfloat16
    power = pl.pallas_call(
        kernel,
        out_shape=jax.ShapeDtypeStruct((HALF, LENGTH), f32),
        in_specs=[anywhere] * (1 + len(constants)),
        out_specs=pl.BlockSpec(memory_space=pltpu.VMEM),
        scratch_shapes=[
            pltpu.VMEM((RAW_ROWS, RAW_COLS), bf16),
            pltpu.VMEM((BLOCK, WIDE), bf16),
            pltpu.VMEM(constants[1].shape, bf16),
            pltpu.VMEM(constants[2].shape, bf16),
            pltpu.VMEM((192, LANES), f32),
            pltpu.VMEM((SLOT, LANES), f32),
            pltpu.VMEM((2 * BLOCK, RAW_COLS + LANES), bf16),
            pltpu.VMEM((BLOCK, WIDE), f32),
            pltpu.VMEM((CORES, SLOT, WIDE), f32),
            pltpu.VMEM((768, 256), f32),
            pltpu.VMEM((2, LANES // 2, 768), f32),
            pltpu.VMEM((2, 2, PAIRS, 384), f32),
            pltpu.VMEM((4, 216, LANES), f32),
            pltpu.VMEM((4, 72, LANES), f32),
            pltpu.VMEM((DEVICES - 1, 6, LANES), f32),
            pltpu.SemaphoreType.DMA((len(CHUNKS) + 5,)),
            pltpu.SemaphoreType.DMA((2,)),
            pltpu.SemaphoreType.DMA((2,)),
            pltpu.SemaphoreType.DMA,
            pltpu.SemaphoreType.DMA,
            pltpu.SemaphoreType.REGULAR,
        ],
        compiler_params=pltpu.CompilerParams(
            collective_id=0, has_side_effects=True, vmem_limit_bytes=54936 * 2**10
        ),
    )(field, *[jnp.asarray(c) for c in constants])
    return power[None]


def solution(mesh):
    return jax.shard_map(
        local,
        mesh=mesh,
        in_specs=(P(None, "rows", "cols"),),
        out_specs=P(None, ("rows", "cols"), None),
        check_vma=False,
    )
```

```python
import jax
import jax.numpy as jnp
import ml_dtypes
import numpy as np
from jax import lax
from jax.experimental import pallas as pl
from jax.experimental.pallas import tpu as pltpu
from jax.sharding import PartitionSpec as P

TAPS = 33
STRIDE = 8
REACH = TAPS // 2
MESH = pl.DeviceIdType.MESH

ROWS, COLS = 32, 4
DEVICES = ROWS * COLS
LENGTH = 2304
RADIX = LENGTH // DEVICES
RAW_ROWS = LENGTH * STRIDE // ROWS
RAW_COLS = LENGTH * STRIDE // COLS
OUT_COLS = RAW_COLS // STRIDE
CORES = 2
HOLD = CORES * RADIX
SLOT = 40
BLOCK = CORES * SLOT
PAIRS = DEVICES // CORES
LANES = 128
WIDE = 5 * LANES
HALF = RADIX // 2


FARTHEST = 74
NEARNESS = 2


def bend(place):
    return (place & 1) + 2 * ((place >> 1) & (1 - (place & 1)))


def hops(device):
    y = (device & 2) + ((device >> 4) & 1)
    return bend((device >> 2) & 3) + bend((device >> 5) & 3) + bend(y)


NEAR_ORIGIN = sorted((d for d in range(DEVICES) if hops(d) <= NEARNESS), key=hops)
GROUP_B = [4 * k for k in range(1, 8)]
GROUP_C = [low + 32 * z for z in (2, 1, 3, 0) for low in (2, 3, 0, 1) if low or z]
CUTS = [0] + [LANES + 1024 * t for t in range(5)] + [RAW_COLS]
CHUNKS = list(zip(CUTS[:-1], CUTS[1:]))


def taps_table():
    tap_ids = np.arange(TAPS, dtype=np.float32)
    shaped = np.sinc((tap_ids - np.float32(REACH)) / np.float32(STRIDE)).astype(np.float32)
    shaped = shaped * (
        np.float32(0.54)
        - np.float32(0.46) * np.cos(np.float32(2 * np.pi) * tap_ids / np.float32(TAPS - 1))
    )
    shaped = shaped / np.sum(shaped)
    return shaped.astype(ml_dtypes.bfloat16).astype(np.float32)


def tap_at(offset):
    taps = taps_table()
    inside = (offset >= 0) & (offset < TAPS)
    return np.where(inside, taps[np.clip(offset, 0, TAPS - 1)], 0).astype(ml_dtypes.bfloat16)


def split(matrix):
    high = matrix.astype(ml_dtypes.bfloat16)
    low = (matrix - high.astype(np.float64)).astype(ml_dtypes.bfloat16)
    return high, low


def tables():
    own = np.full((CORES, SLOT), -(10**6))
    own[:, :HOLD] = HOLD * np.arange(CORES)[:, None] + np.arange(HOLD)
    own[0, HOLD : HOLD + 2] = [-2, -1]
    own[1, HOLD : HOLD + 2] = [CORES * HOLD, CORES * HOLD + 1]
    raw = np.arange(RAW_ROWS)
    row_band = tap_at(raw[None, :] - STRIDE * own.reshape(-1, 1) + REACH)
    row_band = np.pad(row_band, ((0, 192 - BLOCK), (0, WIDE - RAW_ROWS)))

    lane = np.arange(LANES)
    inner = tap_at(np.arange(10 * LANES)[:, None] - LANES - STRIDE * lane[None, :] + REACH)
    edge = tap_at(lane[:, None] - STRIDE * (lane[None, :] - LANES) + REACH)
    col_band = np.concatenate([inner, edge], axis=0)

    def wave(places, count):
        angle = 2 * np.pi / LANES * (places[:, None] * np.arange(count)[None, :] % LANES)
        cos, sin = np.cos(angle), np.sin(angle)
        return np.block([[cos, -sin], [sin, cos]])

    pair = np.arange(PAIRS)
    first = np.concatenate(split(wave(lane, LANES // 2).T), axis=1)
    main = np.concatenate([wave(2 * pair + e, LANES) for e in range(2)], axis=1)
    odd = np.tile(pair % 2, 2)[:, None]
    before = wave(2 * pair - 1, LANES) * (1 - odd)
    after = wave(2 * pair + 2, LANES) * odd
    main_high, main_low = split(main)
    edge_high, edge_low = split(np.concatenate([before, after], axis=1))
    matrices = np.concatenate(
        [first, main_high, main_high, main_low, edge_high, edge_high, edge_low], axis=0
    )

    window = 0.5 - 0.5 * np.cos(2 * np.pi * np.arange(LENGTH) / LENGTH)
    held = own[pair % 2] + (HOLD * CORES) * (pair[:, None] // 2)
    inside = (held >= 0) & (held < LENGTH)
    row_window = np.where(inside, window[np.clip(held, 0, LENGTH - 1)], 0)
    row_window = np.broadcast_to(row_window.reshape(-1, 1), (PAIRS * SLOT, LANES))

    turn = 2 * np.pi / LENGTH * (np.arange(RADIX)[:, None] * lane[None, :])
    later = np.pad(np.stack([np.cos(turn), np.sin(turn)]), ((0, 0), (0, 24 - RADIX), (0, 0)))
    side_tables = []
    for side in range(2):
        sign = np.where(side * np.arange(24) % 2, -1.0, 1.0)[None, :, None]
        start = HALF * LANES * side
        block = window[start : start + HALF * LANES].reshape(HALF, LANES)
        weights = np.zeros((12, LANES))
        weights[:9] = block
        weights[4] = np.where(lane < 66, block[4], 0)
        weights[9] = np.where(lane >= 62, block[4], 0)
        if side == 0:
            weights[10, :2] = window[HALF * LANES : HALF * LANES + 2]
        else:
            weights[11, -2:] = window[HALF * LANES - 2 : HALF * LANES]
        weights = np.repeat(weights, 8, axis=0)
        side_tables.append((later * sign).reshape(-1, LANES))
        side_tables += [later.reshape(-1, LANES), weights]
    floats = np.concatenate([row_window] + side_tables, axis=0)
    return row_band, col_band, matrices, floats.astype(np.float32)


def real_nine(points):
    sums = [points[m] + points[9 - m] for m in range(1, 5)]
    gaps = [points[m] - points[9 - m] for m in range(1, 5)]
    reals, imags = [points[0] + sums[0] + sums[1] + sums[2] + sums[3]], [None]
    for freq in range(1, 5):
        real, imag = points[0], None
        for m in range(1, 5):
            phase = 2 * np.pi * (m * freq % 9) / 9
            real = real + sums[m - 1] * np.float32(np.cos(phase))
            term = gaps[m - 1] * np.float32(-np.sin(phase))
            imag = term if imag is None else imag + term
        reals.append(real)
        imags.append(imag)
    return reals, imags


def folded(points):
    evens = [points[2 * b % 18] for b in range(9)]
    odds = [points[(9 + 2 * b) % 18] for b in range(9)]
    sums, gaps = [], []
    for even, odd in zip(evens, odds):
        if odd is None:
            sums.append(even)
            gaps.append(even)
        elif even is None:
            sums.append(odd)
            gaps.append(-odd)
        else:
            sums.append(even + odd)
            gaps.append(even - odd)
    return real_nine(sums), real_nine(gaps)


def real_eighteen(points):
    both = folded(points)
    out = []
    for freq in range(18):
        reals, imags = both[freq % 2]
        at = freq % 9
        if at == 0:
            out.append((reals[0], None))
        elif at <= 4:
            out.append((reals[at], imags[at]))
        else:
            out.append((reals[9 - at], -imags[9 - at]))
    return out


def complex_eighteen(real_points, imag_points):
    both_real, both_imag = folded(real_points), folded(imag_points)
    out = []
    for freq in range(18):
        (a_re, a_im), (b_re, b_im) = both_real[freq % 2], both_imag[freq % 2]
        at = freq % 9
        if at == 0:
            out.append((a_re[0], b_re[0]))
        elif at <= 4:
            out.append((a_re[at] - b_im[at], a_im[at] + b_re[at]))
        else:
            out.append((a_re[9 - at] + b_im[9 - at], b_re[9 - at] - a_im[9 - at]))
    return out


def halves(value):
    high = value.astype(jnp.bfloat16)
    low = (value - high.astype(jnp.float32)).astype(jnp.bfloat16)
    return high, low


def product(left, right, dims):
    return lax.dot_general(left, right, (dims, ((), ())), preferred_element_type=jnp.float32)


def kernel(
    field, row_band_in, col_band_in, matrices_in, floats_in,
    power,
    raw, row_band, col_band, matrices, common, row_window,
    rowcut, cut, gathered, turned, leaving, arrived, mixed, beyond, filler,
    load_sem, near_send, near_recv, far_send, far_recv, all_ready,
):
    p, q = lax.axis_index("rows"), lax.axis_index("cols")
    me = p * COLS + q
    side, core = q >> 1, q & 1
    pair = p * CORES + core
    def peer(k):
        return (p ^ (k >> 2), q ^ (k & 3))

    small = len(CHUNKS)
    loads = [
        pltpu.make_async_copy(row_band_in.at[pl.ds(0, BLOCK)], row_band, load_sem.at[small]),
        pltpu.make_async_copy(col_band_in, col_band, load_sem.at[small + 1]),
        pltpu.make_async_copy(matrices_in, matrices, load_sem.at[small + 2]),
        pltpu.make_async_copy(
            floats_in.at[pl.ds(pl.multiple_of(pair * SLOT, 8), SLOT)],
            row_window,
            load_sem.at[small + 3],
        ),
        pltpu.make_async_copy(
            floats_in.at[pl.ds(pl.multiple_of(PAIRS * SLOT + side * 192, 8), 192)],
            common,
            load_sem.at[small + 4],
        ),
    ]
    field_loads = [
        pltpu.make_async_copy(
            field.at[0, :, pl.ds(lo, hi - lo)], raw.at[:, pl.ds(lo, hi - lo)], load_sem.at[t]
        )
        for t, (lo, hi) in enumerate(CHUNKS)
    ]
    for copy in loads[:1] + field_loads[:2] + loads[1:2] + field_loads[2:]:
        copy.start()

    def signal(semaphore, device):
        pl.semaphore_signal(semaphore, inc=1, device_id=device, device_id_type=MESH)

    barrier = pltpu.get_barrier_semaphore()
    for k in GROUP_C + GROUP_B:
        signal(barrier, peer(k))

    for row in (360, 384 + 360):
        turned[pl.ds(row, 24), :] = jnp.zeros((24, 256), jnp.float32)

    def row_copy(part, lo, size):
        to = 1 - core
        return pltpu.make_async_remote_copy(
            src_ref=cut.at[pl.ds(pl.multiple_of(to * SLOT, 8), SLOT), pl.ds(lo, size)],
            dst_ref=gathered.at[core, :, pl.ds(lo, size)],
            send_sem=near_send.at[part],
            recv_sem=near_recv.at[part],
            device_id=(p, q ^ 1),
            device_id_type=MESH,
        )

    near = [row_copy(0, 0, 4 * LANES), row_copy(1, 4 * LANES, LANES)]

    def filter_rows(begin, size):
        part = product(row_band[:, :RAW_ROWS], raw[:, pl.ds(begin, size)], ((1,), (0,)))
        high, low = halves(part)
        rowcut[: BLOCK, pl.ds(begin + LANES, size)] = high
        rowcut[BLOCK :, pl.ds(begin + LANES, size)] = low

    rowcut[:, :LANES] = jnp.zeros((2 * BLOCK, LANES), jnp.bfloat16)
    loads[0].wait()
    field_loads[0].wait()
    filter_rows(0, LANES)
    loads[1].wait()

    def step(u):
        begin = pl.multiple_of(1024 * u, LANES)
        chunk = raw.at[:, pl.ds(begin + LANES, 1024)]
        pltpu.make_async_copy(chunk, chunk, load_sem.at[u + 1]).wait()
        filter_rows(begin + LANES, 1024)
        both = product(
            rowcut[:, pl.ds(begin, 10 * LANES)], col_band[: 10 * LANES, :], ((1,), (0,))
        )
        cut[:, pl.ds(pl.multiple_of(LANES * u, LANES), LANES)] = (
            both[: BLOCK] + both[BLOCK :]
        )

    pl.loop(0, 3)(step)
    for copy in loads[2:]:
        copy.start()
    pl.semaphore_wait(barrier, len(GROUP_B + GROUP_C))
    for k in GROUP_B:
        signal(all_ready, peer(k))
    pl.loop(3, 4)(step)
    near[0].start()
    field_loads[5].wait()
    filter_rows(CUTS[5], RAW_COLS - CUTS[5])
    both = product(
        rowcut[:, 4096 : RAW_COLS + LANES], col_band[: RAW_COLS + LANES - 4096, :], ((1,), (0,))
    ) + product(rowcut[:, LANES : 2 * LANES], col_band[10 * LANES :, :], ((1,), (0,)))
    cut[:, 4 * LANES :] = both[: BLOCK] + both[BLOCK :]
    near[1].start()
    gathered[core] = cut[pl.ds(pl.multiple_of(core * SLOT, 8), SLOT), :]
    for copy in loads[2:]:
        copy.wait()
    for copy in near:
        copy.wait_recv()

    @pl.loop(0, SLOT // 8, unroll=True)
    def _(s):
        rows = pl.ds(pl.multiple_of(8 * s, 8), 8)
        mine = row_window[rows, :]
        left, right = gathered[0, rows, :], pltpu.roll(gathered[1, rows, :], 64, 1)

        def weighted(block, t, at):
            weight = common[96 + 8 * at : 104 + 8 * at, :]
            return block[:, LANES * t : LANES * (t + 1)] * mine * weight

        points = [None] * RADIX
        for t in range(4):
            points[t] = weighted(left, t, t)
            points[5 + t] = weighted(right, 1 + t, 5 + t)
        points[4] = weighted(left, 4, 4) + weighted(right, 0, 9)
        points[9] = weighted(right, 0, 10)
        points[17] = weighted(left, 4, 11)
        for freq, (real, imag) in enumerate(real_eighteen(points)):
            half, low = divmod(freq, HALF)
            out = pl.ds(pl.multiple_of(384 * half + 72 * s + 8 * low, 8), 8)
            cos, sin = common[freq : freq + 1, :], common[24 + freq : 25 + freq, :]
            if imag is None:
                turned[out, :LANES] = real * cos
                turned[out, LANES:] = -real * sin
            else:
                turned[out, :LANES] = real * cos + imag * sin
                turned[out, LANES:] = imag * cos - real * sin

    first_high, first_low = matrices[:LANES, :256], matrices[:LANES, 256:]

    def spread(h):
        part = slice(384 * h, 384 * (h + 1))
        high, low = halves(turned[part, :])
        both = (
            product(first_high, low, ((1,), (1,)))
            + product(first_low, high, ((1,), (1,)))
            + product(first_high, high, ((1,), (1,)))
        )
        leaving[0, :, part] = both[: LANES // 2]
        leaving[1, :, part] = both[LANES // 2 :]

    def block_of(other):
        lanes = pl.multiple_of((other & 1) * 384, LANES)
        return leaving.at[:, pl.ds(other >> 1, 1), pl.ds(lanes, 384)]

    landing = arrived.at[side, :, pl.ds(pair, 1), :]

    def far(other):
        pltpu.make_async_remote_copy(
            src_ref=block_of(other),
            dst_ref=landing,
            send_sem=far_send,
            recv_sem=far_recv,
            device_id=(other >> 2, other & 3),
            device_id_type=MESH,
        ).start()

    for h in (1, 0):
        spread(h)
        if h == 1:
            pl.semaphore_wait(all_ready, len(GROUP_B))
        for first in NEAR_ORIGIN:
            if first % 2 != h:
                continue

            @pl.when(me != first)
            def _():
                far(jnp.int32(first))

    @pl.loop(0, DEVICES)
    def _(step):
        other = me ^ step ^ FARTHEST

        @pl.when((hops(other) > NEARNESS) & (other != me))
        def _():
            far(other)

    pltpu.make_async_copy(block_of(me), landing, far_recv).start()
    pltpu.make_async_copy(arrived, arrived, far_recv).wait()

    high, low = halves((arrived[0] + arrived[1]).reshape(2 * PAIRS, 384).T)
    both = jnp.concatenate([high, low], axis=1)
    for e in range(2):
        rows, lanes = slice(144 * e, 144 * e + 216), slice(256 * e, 256 * e + 256)
        total = product(both[rows], matrices[128:384, lanes], ((1,), (0,))) + product(
            high[rows], matrices[384:512, lanes], ((1,), (0,))
        )
        mixed[2 * e], mixed[2 * e + 1] = total[:, :LANES], total[:, LANES:]
    rest = product(both[288:360], matrices[512:768, :], ((1,), (0,))) + product(
        high[288:360], matrices[768:896, :], ((1,), (0,))
    )
    for t in range(4):
        beyond[t] = rest[:, LANES * t : LANES * (t + 1)]

    def held(e, part, slot):
        row = 72 * (slot // 8) + slot % 8 - 144 * e
        return mixed[2 * e + part, pl.ds(row, HALF, stride=8), :]

    real_points, imag_points = [], []
    for r in range(RADIX):
        real, imag = (held(0, part, r) + held(1, part, RADIX + r) for part in range(2))
        if r < 2:
            real = real + beyond[2, pl.ds(4 + r, HALF, stride=8), :]
            imag = imag + beyond[3, pl.ds(4 + r, HALF, stride=8), :]
        if r >= RADIX - 2:
            real = real + beyond[0, pl.ds(4 + r - (RADIX - 2), HALF, stride=8), :]
            imag = imag + beyond[1, pl.ds(4 + r - (RADIX - 2), HALF, stride=8), :]
        cos, sin = common[48 + r : 49 + r, :], common[72 + r : 73 + r, :]
        real_points.append(real * cos + imag * sin)
        imag_points.append(imag * cos - real * sin)
    for freq, (real, imag) in enumerate(complex_eighteen(real_points, imag_points)):
        power[:, 0, LANES * freq : LANES * (freq + 1)] = (real * real + imag * imag) * np.float32(
            8.0 / (LENGTH * LENGTH)
        )

    for copy in near:
        copy.wait_send()
    pltpu.make_async_copy(filler, filler, far_send).wait()


def local(field):
    constants = tables()
    anywhere = pl.BlockSpec(memory_space=pltpu.HBM)
    f32, bf16 = jnp.float32, jnp.bfloat16
    power = pl.pallas_call(
        kernel,
        out_shape=jax.ShapeDtypeStruct((HALF, 1, LENGTH), f32),
        in_specs=[anywhere] * (1 + len(constants)),
        out_specs=pl.BlockSpec(memory_space=pltpu.VMEM),
        scratch_shapes=[
            pltpu.VMEM((RAW_ROWS, RAW_COLS), bf16),
            pltpu.VMEM((BLOCK, WIDE), bf16),
            pltpu.VMEM(constants[1].shape, bf16),
            pltpu.VMEM(constants[2].shape, bf16),
            pltpu.VMEM((192, LANES), f32),
            pltpu.VMEM((SLOT, LANES), f32),
            pltpu.VMEM((2 * BLOCK, RAW_COLS + LANES), bf16),
            pltpu.VMEM((BLOCK, WIDE), f32),
            pltpu.VMEM((CORES, SLOT, WIDE), f32),
            pltpu.VMEM((768, 256), f32),
            pltpu.VMEM((2, LANES // 2, 768), f32),
            pltpu.VMEM((2, 2, PAIRS, 384), f32),
            pltpu.VMEM((4, 216, LANES), f32),
            pltpu.VMEM((4, 72, LANES), f32),
            pltpu.VMEM((DEVICES - 1, 6, LANES), f32),
            pltpu.SemaphoreType.DMA((len(CHUNKS) + 5,)),
            pltpu.SemaphoreType.DMA((2,)),
            pltpu.SemaphoreType.DMA((2,)),
            pltpu.SemaphoreType.DMA,
            pltpu.SemaphoreType.DMA,
            pltpu.SemaphoreType.REGULAR,
        ],
        compiler_params=pltpu.CompilerParams(
            collective_id=0, has_side_effects=True, vmem_limit_bytes=54936 * 2**10
        ),
    )(field, *[jnp.asarray(c) for c in constants])
    return power.reshape(1, HALF, LENGTH)


def solution(mesh):
    return jax.shard_map(
        local,
        mesh=mesh,
        in_specs=(P(None, "rows", "cols"),),
        out_specs=P(None, ("rows", "cols"), None),
        check_vma=False,
    )
```
